32 devices in a mesh: row: 2 (over x), col: 4 (over z), grp: 4 (over y, core).
Axes of the slice: x: 2, y: 2, z: 4, core: 2. Of those that a mesh axis runs over, the one named last changes fastest.
Arguments:
- tokens: bfloat16 [8, 256, 2048], P(('grp', 'row'), None, 'col'), may hold values from -8 to 8
- w_query: bfloat16 [2048, 2048], P(None, 'col'), may hold values from -0.125 to 0.125
- w_key: bfloat16 [2048, 2048], P(None, 'col'), may hold values from -0.125 to 0.125
- w_value: bfloat16 [2048, 2048], P(None, 'col'), may hold values from -0.125 to 0.125
- w_out: bfloat16 [2048, 2048], P('col'), may hold values from -0.125 to 0.125
- diff_lambda: float32 [8], replicated, may hold values from 0.2 to 0.8
- prefix_keys: bfloat16 [8, 4, 256, 2048], P(('grp', 'row'), None, None, 'col'), may hold values from -800 to 800
- prefix_values: bfloat16 [8, 4, 256, 2048], P(('grp', 'row'), None, None, 'col'), may hold values from -6 to 6
- new_len: int32 [8], P(('grp', 'row')), may hold values from 64 to 256
- prefix_len: int32 [8], P(('grp', 'row')), may hold values from 0 to 1024, as said below
- holder: int32 [8, 4], P(('grp', 'row')), may hold values from 0 to 3, as said below
- page_table: int32 [8, 4], replicated, may hold values from 0 to 3, as said below
Outputs:
- hidden: bfloat16 [8, 256, 2048], P(('grp', 'row'), None, 'col')
- page_keys: bfloat16 [4, 2, 4, 64, 2048], P('grp', 'row', None, None, 'col')
- page_values: bfloat16 [4, 2, 4, 64, 2048], P('grp', 'row', None, None, 'col')
The draws below stay inside these ranges and needn't reach their ends.
Inputs may be any that keep to these rules, and one draw needn't show every extreme that they name: `prefix_len`: half of the requests have no prefix; one has exactly 1024. Each row of holder names every group once. For each r and b, the entries page_table[g * 2 + r, b] over the 4 groups g name every slot once.
All inputs are finite; a program needn't handle non-finite values.
Results may differ from the reference program's by a relative error of at most 0.0078.
Values may be sent and summed in bfloat16 or wider, within the bound.
A program may use at most 64 MiB of HBM per device.

```python
import math
import jax
import jax.numpy as jnp
from jax import lax

D = 2048
HEADS = 8
DK = 128
DV = 256
NEWTOK = 256
PMAX = 1024
GROUPS = 4
ROWS = 2
REQS = 8
PAGE = 64
PBLOCK = 256


def draw_tokens(key, part):
    key_base, key_rows = jax.random.split(key, 2)
    base_draw = jax.random.normal(key_base, (REQS, NEWTOK, D), jnp.float32)
    row_scale = jnp.exp(jax.random.uniform(key_rows, (REQS, NEWTOK, 1), jnp.float32, math.log(0.5), math.log(2.0)))
    drawn = base_draw * row_scale
    return jnp.clip(drawn, -8.0, 8.0).astype(jnp.bfloat16)


def draw_prefix_keys(key, part):
    key_base = jax.random.fold_in(key, 0)
    base_draw = jnp.clip(jax.random.normal(key_base, (REQS, GROUPS, PBLOCK, 2 * HEADS * DK), jnp.float32), -8.0, 8.0)
    return base_draw.astype(jnp.bfloat16)


def draw_prefix_len(key, part):
    key_order, key_len = jax.random.split(key, 2)
    shuffled = jax.random.permutation(key_order, REQS)
    lengths = jax.random.randint(key_len, (REQS,), 1, PMAX + 1)
    lengths = lengths.at[shuffled[0]].set(PMAX)
    with_prefix = jnp.zeros((REQS,), jnp.int32).at[shuffled[:REQS // 2]].set(1)
    return jnp.where(with_prefix == 1, lengths, 0).astype(jnp.int32)


def draw_holder(key, part):
    sub_keys = jax.random.split(key, REQS)
    return jax.vmap(lambda sub_key: jax.random.permutation(sub_key, GROUPS))(sub_keys).astype(jnp.int32)


def draw_page_table(key, part):
    sub_keys = jax.random.split(key, ROWS * GROUPS)
    shuffled = jax.vmap(lambda sub_key: jax.random.permutation(sub_key, GROUPS))(sub_keys).reshape(ROWS, GROUPS, GROUPS)
    return jnp.transpose(shuffled, (2, 0, 1)).reshape(REQS, GROUPS).astype(jnp.int32)


def with_ends(entries, rng, low, largest):
    longest = entries.shape.index(max(entries.shape))
    spots = []
    for shift in (0, 1):
        where = [jax.random.randint(jax.random.fold_in(rng, axis), (), 0, length) for axis, length in enumerate(entries.shape)]
        where[longest] = (where[longest] + shift) % entries.shape[longest]
        spots.append(tuple(where))
    return entries.at[spots[0]].set(low).at[spots[1]].set(largest)


def level_of(own_key, shape, pieces, least, top_value):
    factor_of, own = 1.0, jax.random.fold_in(own_key, 6)
    for axis_at, blocks in pieces:
        steps = jnp.exp(jax.random.uniform(jax.random.fold_in(own, axis_at), (blocks,), jnp.float32, least / len(pieces), top_value / len(pieces)))
        factor_of = factor_of * jnp.repeat(steps, shape[axis_at] // blocks).reshape([-1 if axis == axis_at else 1 for axis in range(len(shape))])
    return factor_of


def gaussian(key, shape, scale, reach, cuts=(), kind=jnp.bfloat16):
    entries = jax.random.normal(key, shape, jnp.float32) * scale
    if len(cuts) > 0:
        entries = level_of(key, shape, cuts, -0.22, 0.18) * entries
    return jnp.clip(entries, min=-reach, max=reach).astype(kind)


def setup_inputs(seed: int = 0) -> dict:
    seeds = jax.random.split(jax.random.key(seed), 13)
    return {
        "tokens": draw_tokens(jax.random.fold_in(seeds[12], 71), 0),
        "w_query": gaussian(seeds[1], (D, 2 * HEADS * DK), D ** -0.5, 0.125, ((1, 4),)),
        "w_key": gaussian(seeds[2], (D, 2 * HEADS * DK), D ** -0.5, 0.125, ((1, 4),)),
        "w_value": gaussian(seeds[3], (D, HEADS * DV), D ** -0.5, 0.125, ((1, 4),)),
        "w_out": gaussian(seeds[4], (HEADS * DV, D), (HEADS * DV) ** -0.5, 0.125, ((0, 4),)),
        "diff_lambda": jnp.clip(jax.random.uniform(seeds[5], (HEADS,), jnp.float32, 0.2, 0.8), 0.2, 0.8),
        "prefix_keys": draw_prefix_keys(jax.random.fold_in(seeds[12], 71), 0),
        "prefix_values": gaussian(seeds[7], (REQS, GROUPS, PBLOCK, HEADS * DV), 1.0, 6.0, ((0, 8), (3, 4))),
        "new_len": with_ends(jax.random.randint(seeds[8], (REQS,), NEWTOK // 4, NEWTOK + 1), jax.random.fold_in(seeds[8], 1), NEWTOK // 4, NEWTOK).astype(jnp.int32),
        "prefix_len": draw_prefix_len(jax.random.fold_in(seeds[12], 71), 0),
        "holder": draw_holder(jax.random.fold_in(seeds[12], 71), 0),
        "page_table": draw_page_table(jax.random.fold_in(seeds[12], 71), 0),
    }


EPS_INPUT = 1e-06
EPS_HEAD = 1e-05
OUT_SCALE = 0.8

def head_attend(queries_in, key_set, value_set, allowed):
    scores = jnp.einsum('chd,khd->hck', queries_in.astype(jnp.float32), key_set.astype(jnp.float32), precision=lax.Precision.HIGHEST) * queries_in.shape[-1] ** (-0.5)
    scores = jnp.where(allowed[None], scores, -jnp.inf)
    highest = lax.optimization_barrier(jnp.max(scores, axis=-1, keepdims=True))
    exp_scores = jnp.exp(scores - highest)
    weights = (exp_scores / lax.optimization_barrier(jnp.sum(exp_scores, axis=-1, keepdims=True))).astype(jnp.bfloat16)
    return jnp.einsum('hck,khe->che', weights.astype(jnp.float32), value_set.astype(jnp.float32), precision=lax.Precision.HIGHEST)

def project(flat, inv_rms, weight):
    return (jnp.dot(flat, weight.astype(jnp.float32), precision=lax.Precision.HIGHEST) * inv_rms).astype(jnp.bfloat16)

def reference(tokens, w_query, w_key, w_value, w_out, diff_lambda, prefix_keys, prefix_values, new_len, prefix_len, holder, page_table):
    flat = tokens.reshape(REQS * NEWTOK, D).astype(jnp.float32)
    inv_rms = lax.rsqrt(lax.optimization_barrier(jnp.mean(flat * flat, axis=1, keepdims=True)) + EPS_INPUT)
    queries = project(flat, inv_rms, w_query).reshape(REQS, NEWTOK, HEADS, 2, DK)
    new_keys = project(flat, inv_rms, w_key)
    new_values = project(flat, inv_rms, w_value)
    keys_heads = new_keys.reshape(REQS, NEWTOK, HEADS, 2, DK)
    values_heads = new_values.reshape(REQS, NEWTOK, HEADS, DV)
    request = jnp.arange(REQS, dtype=jnp.int32)
    source = holder * ROWS + (request % ROWS)[:, None]
    asker = jnp.broadcast_to((request // ROWS)[:, None], (REQS, GROUPS))
    fetched_keys = prefix_keys[source, asker].reshape(REQS, PMAX, HEADS, 2, DK)
    fetched_values = prefix_values[source, asker].reshape(REQS, PMAX, HEADS, DV)
    position = jnp.arange(PMAX + NEWTOK, dtype=jnp.int32)
    within = jnp.arange(NEWTOK, dtype=jnp.int32)

    def one_request(index):
        key_set = jnp.concatenate([fetched_keys[index], keys_heads[index]], axis=0)
        value_set = jnp.concatenate([fetched_values[index], values_heads[index]], axis=0)
        allowed = jnp.where(position[None, :] < PMAX, position[None, :] < prefix_len[index], position[None, :] - PMAX <= within[:, None])
        own_queries = queries[index]
        map_zero = head_attend(own_queries[:, :, 0], key_set[:, :, 0], value_set, allowed)
        map_one = head_attend(own_queries[:, :, 1], key_set[:, :, 1], value_set, allowed)
        differ = map_zero - diff_lambda[None, :, None] * map_one
        normed = OUT_SCALE * differ * lax.rsqrt(lax.optimization_barrier(jnp.mean(differ * differ, axis=-1, keepdims=True)) + EPS_HEAD)
        return normed.astype(jnp.bfloat16).reshape(NEWTOK, HEADS * DV)
    attended = lax.map(one_request, request)
    mixed = jnp.dot(attended.reshape(REQS * NEWTOK, HEADS * DV).astype(jnp.float32), w_out.astype(jnp.float32), precision=lax.Precision.HIGHEST)
    is_live = within[None, :] < new_len[:, None]
    summed = tokens.astype(jnp.float32) + mixed.reshape(REQS, NEWTOK, D)
    hidden = jnp.where(is_live[:, :, None], summed, 0.0).astype(jnp.bfloat16)
    table = page_table.reshape(GROUPS, ROWS, GROUPS)
    placed = (table[..., None] == jnp.arange(GROUPS, dtype=jnp.int32)).astype(jnp.float32)

    def to_pages(field, width):
        kept = jnp.where(is_live[:, :, None], field.reshape(REQS, NEWTOK, width).astype(jnp.float32), 0.0)
        blocks = kept.reshape(GROUPS, ROWS, GROUPS, PAGE, width)
        return jnp.einsum('grbs,grbpc->brspc', placed, blocks, precision=lax.Precision.HIGHEST).astype(jnp.bfloat16)
    return (hidden, to_pages(new_keys, 2 * HEADS * DK), to_pages(new_values, HEADS * DV))
```

```python
import functools
import jax
import jax.numpy as jnp
from jax import lax
from jax.experimental import pallas as pl
from jax.experimental.pallas import tpu as pltpu
from jax.sharding import PartitionSpec as P

D = 2048
DK = 128
DV = 256


EPS_INPUT = 1e-06
EPS_HEAD = 1e-05
OUT_SCALE = 0.8


def swapped(x, axis, stride):
    return lax.ppermute(x, axis, [(i, i ^ 1 << stride) for i in range(lax.axis_size(axis))])


def head_attend(queries_in, key_set, value_set, allowed):
    scores = jnp.einsum(
        "chd,khd->hck", queries_in, key_set, preferred_element_type=jnp.float32
    ) * queries_in.shape[-1] ** (-0.5)
    scores = jnp.where(allowed[None], scores, -jnp.inf)
    highest = jnp.max(scores, axis=-1, keepdims=True)
    exp_scores = jnp.exp(scores - highest)
    weights = (exp_scores / jnp.sum(exp_scores, axis=-1, keepdims=True)).astype(jnp.bfloat16)
    return jnp.einsum("hck,khe->che", weights, value_set, preferred_element_type=jnp.float32)


def arrange(is_first, own_part, other_part):
    return (jnp.where(is_first, own_part, other_part), jnp.where(is_first, other_part, own_part))


def head_norm(differ):
    return (
        OUT_SCALE * differ * lax.rsqrt(jnp.mean(differ * differ, axis=-1, keepdims=True) + EPS_HEAD)
    )


MASKED = -1e30
LOG2E = 1.4426950408889634


def fits_kernel(w_query, prefix_keys):
    return w_query.shape[1] % (2 * DK) == 0 and lax.axis_size("grp") == 4


def kernel(
    n_col,
    n_row,
    new_len,
    prefix_len,
    holder,
    page_table,
    diff_lambda,
    tokens,
    w_query,
    w_key,
    w_value,
    w_out,
    prefix_keys,
    prefix_values,
    hidden,
    page_keys,
    page_values,
    tok,
    weights,
    w_last,
    kbuf,
    vbuf,
    sums,
    queries,
    acc,
    top,
    low,
    attended,
    outgoing,
    incoming,
    page_out,
    page_in,
    local_sem,
    tok_send,
    tok_recv,
    pre_send,
    pre_recv,
    page_send,
    page_recv,
    mix_send,
    mix_recv,
):
    groups = 4
    grp = lax.axis_index("grp")
    row = lax.axis_index("row")
    col = lax.axis_index("col")
    slots, cols = tok.shape[1], tok.shape[2]
    heads = queries.shape[1] // (2 * DK)
    block = kbuf.shape[1]
    page = slots // groups
    peers = (None, grp + 1 - 2 * lax.rem(grp, 2), lax.rem(grp + 2, groups), groups - 1 - grp)

    def ahead(step):
        return lax.rem(col + step, n_col)

    def behind(step):
        return lax.rem(col + n_col - step, n_col)

    copies = [
        pltpu.make_async_copy(tokens.at[0], tok.at[0], local_sem.at[0]),
        pltpu.make_async_copy(w_query, weights.at[0], local_sem.at[1]),
        pltpu.make_async_copy(w_key, weights.at[1], local_sem.at[2]),
        pltpu.make_async_copy(w_value, weights.at[2], local_sem.at[3]),
        pltpu.make_async_copy(prefix_keys.at[0, grp], kbuf.at[0], local_sem.at[4]),
        pltpu.make_async_copy(prefix_values.at[0, grp], vbuf.at[0], local_sem.at[5]),
        pltpu.make_async_copy(w_out, w_last, local_sem.at[6]),
    ]
    barrier = pltpu.get_barrier_semaphore()
    for step in range(1, n_col):
        pl.semaphore_signal(
            barrier, inc=1, device_id={"col": ahead(step)}, device_id_type=pl.DeviceIdType.MESH
        )
    for step in range(1, groups):
        pl.semaphore_signal(
            barrier, inc=1, device_id={"grp": peers[step]}, device_id_type=pl.DeviceIdType.MESH
        )
    for copy in copies:
        copy.start()
    pl.semaphore_wait(barrier, n_col - 1 + groups - 1)

    def remote(source, target, send, recv, where):
        return pltpu.make_async_remote_copy(
            src_ref=source,
            dst_ref=target,
            send_sem=send,
            recv_sem=recv,
            device_id=where,
            device_id_type=pl.DeviceIdType.MESH,
        )

    token_copies = [None] + [
        remote(tokens.at[0], tok.at[step], tok_send.at[step], tok_recv.at[step], {"col": ahead(step)})
        for step in range(1, n_col)
    ]
    for step in range(1, n_col):
        token_copies[step].start()
    key_copies, value_copies = [None], [None]
    for step in range(1, groups):
        peer = peers[step]
        key_copies.append(
            remote(
                prefix_keys.at[0, peer], kbuf.at[step], pre_send.at[0, step], pre_recv.at[0, step], {"grp": peer}
            )
        )
        value_copies.append(
            remote(
                prefix_values.at[0, peer], vbuf.at[step], pre_send.at[1, step], pre_recv.at[1, step], {"grp": peer}
            )
        )
    for step in (2, 3, 1):
        key_copies[step].start()
        value_copies[step].start()

    for copy in copies[:4]:
        copy.wait()
    square = jnp.zeros((slots, 1), jnp.float32)
    for step in range(n_col):
        if step:
            token_copies[step].wait_recv()
        shard = tok[step]
        as_float = shard.astype(jnp.float32)
        square = square + jnp.sum(as_float * as_float, axis=1, keepdims=True)
        first = pl.multiple_of(behind(step) * cols, cols)
        for which in range(3):
            part = jnp.dot(
                shard, weights[which, pl.ds(first, cols), :], preferred_element_type=jnp.float32
            )
            if step:
                part = part + sums[which]
            sums[which] = part
    inv_rms = lax.rsqrt(square / D + EPS_INPUT)
    live = lax.broadcasted_iota(jnp.int32, (slots, 1), 0) < new_len[0]
    queries[...] = (sums[0] * inv_rms).astype(jnp.bfloat16)
    new_keys = (sums[1] * inv_rms).astype(jnp.bfloat16)
    new_values = (sums[2] * inv_rms).astype(jnp.bfloat16)
    kbuf[groups] = new_keys
    vbuf[groups] = new_values
    page_out[0] = jnp.where(live, new_keys, jnp.zeros_like(new_keys))
    page_out[1] = jnp.where(live, new_values, jnp.zeros_like(new_values))

    scale = DK**-0.5 * LOG2E
    key_at = lax.broadcasted_iota(jnp.int32, (slots, block), 1)
    query_at = lax.broadcasted_iota(jnp.int32, (slots, block), 0)

    def attend(index, allowed, first):
        def one_head(head):
            value = vbuf[index, :, head * DV : (head + 1) * DV]
            for which in range(2):
                at = head * 2 + which
                scores = lax.dot_general(
                    queries[:, at * DK : (at + 1) * DK],
                    kbuf[index, :, at * DK : (at + 1) * DK],
                    (((1,), (1,)), ((), ())),
                    preferred_element_type=jnp.float32,
                )
                scores = jnp.where(allowed, scores * scale, MASKED)
                highest = jnp.max(scores, axis=1, keepdims=True)
                if not first:
                    before = top[at]
                    highest = jnp.maximum(before, highest)
                weight = jnp.exp2(scores - highest)
                total = jnp.sum(weight, axis=1, keepdims=True)
                mixed = jnp.dot(weight.astype(jnp.bfloat16), value, preferred_element_type=jnp.float32)
                if not first:
                    decay = jnp.exp2(before - highest)
                    total = total + low[at] * decay
                    mixed = mixed + acc[at] * decay
                top[at] = highest
                low[at] = total
                acc[at] = mixed

        for head in range(heads):
            one_head(head)

    attend(groups, key_at <= query_at, True)
    for step in range(groups):
        if step:
            key_copies[step].wait_recv()
            value_copies[step].wait_recv()
        else:
            copies[4].wait()
            copies[5].wait()
        source = peers[step] if step else grp
        place = jnp.int32(0)
        for at in range(groups):
            place = jnp.where(holder[0, at] == source, at, place)
        attend(step, key_at < prefix_len[0] - place * block, False)

    for head in range(heads):
        zero, one = 2 * head, 2 * head + 1
        differ = acc[zero] / low[zero] - diff_lambda[col * heads + head] * (acc[one] / low[one])
        normed = OUT_SCALE * differ * lax.rsqrt(jnp.mean(differ * differ, axis=1, keepdims=True) + EPS_HEAD)
        attended[:, head * DV : (head + 1) * DV] = normed.astype(jnp.bfloat16)

    copies[6].wait()

    def share(step):
        first = pl.multiple_of(ahead(step) * cols, cols)
        return jnp.dot(attended[...], w_last[:, pl.ds(first, cols)], preferred_element_type=jnp.float32)

    mix_copies = [None]
    for step in range(1, n_col):
        outgoing[step] = share(step).astype(jnp.bfloat16)
        copy = remote(
            outgoing.at[step], incoming.at[step], mix_send.at[step], mix_recv.at[step], {"col": ahead(step)}
        )
        copy.start()
        mix_copies.append(copy)

    page_copies = []
    for step in range(1, groups):
        peer = peers[step]
        rows = pl.ds(pl.multiple_of(peer * page, page), page)
        for kind in range(2):
            copy = remote(
                page_out.at[kind, rows],
                page_in.at[kind, grp],
                page_send.at[kind, step],
                page_recv.at[kind, step],
                {"grp": peer},
            )
            copy.start()
            page_copies.append(copy)
    for kind in range(2):
        page_in[kind, grp] = page_out[kind, pl.ds(pl.multiple_of(grp * page, page), page), :]

    total = share(0) + tok[0].astype(jnp.float32)
    for copy in page_copies:
        copy.wait_recv()
    for slot in range(groups):
        source = jnp.int32(0)
        for at in range(groups):
            source = jnp.where(page_table[at * n_row + row, grp] == slot, at, source)
        page_keys[0, 0, slot] = page_in[0, source]
        page_values[0, 0, slot] = page_in[1, source]
    for step in range(1, n_col):
        mix_copies[step].wait_recv()
        total = total + incoming[step].astype(jnp.float32)
    hidden[0] = jnp.where(live, total, 0.0).astype(jnp.bfloat16)
    for copy in token_copies[1:] + key_copies[1:] + value_copies[1:] + page_copies + mix_copies[1:]:
        copy.wait_send()


def fused(
    tokens,
    w_query,
    w_key,
    w_value,
    w_out,
    diff_lambda,
    prefix_keys,
    prefix_values,
    new_len,
    prefix_len,
    holder,
    page_table,
):
    n_col, n_row, groups = lax.axis_size("col"), lax.axis_size("row"), lax.axis_size("grp")
    slots, cols = tokens.shape[1:]
    depth, wide = w_query.shape
    block = prefix_keys.shape[2]
    page = slots // groups
    maps = wide // DK
    scalars = pl.BlockSpec(memory_space=pltpu.SMEM)
    remains = pl.BlockSpec(memory_space=pl.ANY)
    whole = pl.BlockSpec(memory_space=pltpu.VMEM)
    half, full = jnp.bfloat16, jnp.float32
    return pl.pallas_call(
        functools.partial(kernel, n_col, n_row),
        out_shape=(
            jax.ShapeDtypeStruct((1, slots, cols), half),
            jax.ShapeDtypeStruct((1, 1, groups, page, wide), half),
            jax.ShapeDtypeStruct((1, 1, groups, page, wide), half),
        ),
        in_specs=[scalars] * 5 + [remains] * 7,
        out_specs=(whole, whole, whole),
        scratch_shapes=[
            pltpu.VMEM((n_col, slots, cols), half),
            pltpu.VMEM((3, depth, wide), half),
            pltpu.VMEM(w_out.shape, half),
            pltpu.VMEM((groups + 1, block, wide), half),
            pltpu.VMEM((groups + 1, block, wide), half),
            pltpu.VMEM((3, slots, wide), full),
            pltpu.VMEM((slots, wide), half),
            pltpu.VMEM((maps, slots, DV), full),
            pltpu.VMEM((maps, slots, 1), full),
            pltpu.VMEM((maps, slots, 1), full),
            pltpu.VMEM((slots, wide), half),
            pltpu.VMEM((n_col, slots, cols), half),
            pltpu.VMEM((n_col, slots, cols), half),
            pltpu.VMEM((2, slots, wide), half),
            pltpu.VMEM((2, groups, page, wide), half),
            pltpu.SemaphoreType.DMA((7,)),
            pltpu.SemaphoreType.DMA((n_col,)),
            pltpu.SemaphoreType.DMA((n_col,)),
            pltpu.SemaphoreType.DMA((2, groups)),
            pltpu.SemaphoreType.DMA((2, groups)),
            pltpu.SemaphoreType.DMA((2, groups)),
            pltpu.SemaphoreType.DMA((2, groups)),
            pltpu.SemaphoreType.DMA((n_col,)),
            pltpu.SemaphoreType.DMA((n_col,)),
        ],
        compiler_params=pltpu.CompilerParams(
            collective_id=0, has_side_effects=True, vmem_limit_bytes=48 << 20
        ),
    )(
        new_len,
        prefix_len,
        holder,
        page_table,
        diff_lambda,
        tokens,
        w_query,
        w_key,
        w_value,
        w_out,
        prefix_keys,
        prefix_values,
    )


def local(
    tokens,
    w_query,
    w_key,
    w_value,
    w_out,
    diff_lambda,
    prefix_keys,
    prefix_values,
    new_len,
    prefix_len,
    holder,
    page_table,
):
    if fits_kernel(w_query, prefix_keys):
        return fused(
            tokens,
            w_query,
            w_key,
            w_value,
            w_out,
            diff_lambda,
            prefix_keys,
            prefix_values,
            new_len,
            prefix_len,
            holder,
            page_table,
        )
    groups = lax.axis_size("grp")
    row_count = lax.axis_size("row")
    grp_index = lax.axis_index("grp")
    row_index = lax.axis_index("row")
    col_index = lax.axis_index("col")
    local_tokens = tokens[0]
    slot_count = local_tokens.shape[0]
    query_cols = w_query.shape[1]
    value_cols = w_value.shape[1]
    group_ids = jnp.arange(groups, dtype=jnp.int32)
    got_keys, got_values = (
        lax.all_to_all(prefix_keys[0], "grp", split_axis=0, concat_axis=0, tiled=True),
        lax.all_to_all(prefix_values[0], "grp", split_axis=0, concat_axis=0, tiled=True),
    )
    shard_piece = lax.all_gather(local_tokens, "col", axis=1, tiled=True)

    def partial_product(weight):
        return jnp.dot(shard_piece, weight, preferred_element_type=jnp.float32)

    as_float = shard_piece.astype(jnp.float32)
    query_sum = partial_product(w_query)
    key_sum = partial_product(w_key)
    value_sum = partial_product(w_value)
    square_sum = jnp.sum(as_float * as_float, axis=1)
    inv_rms = lax.rsqrt(square_sum / D + EPS_INPUT)[:, None]
    queries = (query_sum * inv_rms).astype(jnp.bfloat16)
    new_keys = (key_sum * inv_rms).astype(jnp.bfloat16)
    new_values = (value_sum * inv_rms).astype(jnp.bfloat16)
    is_live = jnp.arange(slot_count) < new_len[0]
    zero_entry = jnp.zeros((), jnp.bfloat16)
    page_size = slot_count // groups
    send_keys = jnp.where(is_live[:, None], new_keys, zero_entry).reshape(
        groups, page_size, query_cols
    )
    send_values = jnp.where(is_live[:, None], new_values, zero_entry).reshape(
        groups, page_size, value_cols
    )
    recv_keys, recv_values = (
        lax.all_to_all(send_keys, "grp", split_axis=0, concat_axis=0, tiled=True),
        lax.all_to_all(send_values, "grp", split_axis=0, concat_axis=0, tiled=True),
    )
    pick_block = (holder[0][:, None] == group_ids[None, :]).astype(jnp.bfloat16)
    fetched_keys = (
        jnp.einsum("bh,hpc->bpc", pick_block, got_keys, preferred_element_type=jnp.float32)
        .astype(jnp.bfloat16)
        .reshape(-1, query_cols)
    )
    fetched_values = (
        jnp.einsum("bh,hpc->bpc", pick_block, got_values, preferred_element_type=jnp.float32)
        .astype(jnp.bfloat16)
        .reshape(-1, value_cols)
    )
    prefix_span = fetched_keys.shape[0]
    position = jnp.arange(prefix_span + slot_count)
    within = jnp.arange(slot_count)
    allowed = jnp.where(
        position[None, :] < prefix_span,
        position[None, :] < prefix_len[0],
        position[None, :] - prefix_span <= within[:, None],
    )
    key_own = jnp.concatenate([fetched_keys, new_keys], axis=0)
    value_own = jnp.concatenate([fetched_values, new_values], axis=0)
    if query_cols == DK:
        is_first = col_index % 2 == 0
        head_lam = diff_lambda[col_index // 2]
        half_width = DV // 2
        partner_query, partner_key, partner_value, partner_pkey, partner_pvalue = swapped(
            (queries, new_keys, new_values, fetched_keys, fetched_values), "col", 0
        )
        query_zero, query_one = arrange(is_first, queries, partner_query)
        key_zero, key_one = arrange(
            is_first, key_own, jnp.concatenate([partner_pkey, partner_key], axis=0)
        )
        value_low, value_high = arrange(
            is_first, value_own, jnp.concatenate([partner_pvalue, partner_value], axis=0)
        )
        value_full = jnp.concatenate([value_low, value_high], axis=1)[:, None, :]
        map_zero = head_attend(query_zero[:, None, :], key_zero[:, None, :], value_full, allowed)
        map_one = head_attend(query_one[:, None, :], key_one[:, None, :], value_full, allowed)
        normed = head_norm(map_zero - head_lam * map_one)
        attended = lax.dynamic_slice_in_dim(
            normed[:, 0, :], col_index % 2 * half_width, half_width, 1
        ).astype(jnp.bfloat16)
    else:
        local_heads = query_cols // (2 * DK)
        query_four = queries.reshape(slot_count, local_heads, 2, DK)
        key_four = key_own.reshape(-1, local_heads, 2, DK)
        value_three = value_own.reshape(-1, local_heads, DV)
        map_zero = head_attend(query_four[:, :, 0], key_four[:, :, 0], value_three, allowed)
        map_one = head_attend(query_four[:, :, 1], key_four[:, :, 1], value_three, allowed)
        head_lam = lax.dynamic_slice_in_dim(diff_lambda, col_index * local_heads, local_heads, 0)
        normed = head_norm(map_zero - head_lam[None, :, None] * map_one)
        attended = normed.reshape(slot_count, local_heads * DV).astype(jnp.bfloat16)
    mixed = lax.psum_scatter(
        lax.dot_general(
            w_out, attended, (((0,), (1,)), ((), ())), preferred_element_type=jnp.float32
        ),
        "col",
        scatter_dimension=0,
        tiled=True,
    ).T
    combined = local_tokens.astype(jnp.float32) + mixed
    hidden = jnp.where(is_live[:, None], combined, 0.0).astype(jnp.bfloat16)[None]
    sources = group_ids * row_count + row_index
    slot_of = page_table[sources, grp_index]
    placement_map = (slot_of[None, :] == group_ids[:, None]).astype(jnp.bfloat16)
    page_keys = jnp.einsum(
        "sg,gpc->spc", placement_map, recv_keys, preferred_element_type=jnp.float32
    ).astype(jnp.bfloat16)[None, None]
    page_values = jnp.einsum(
        "sg,gpc->spc", placement_map, recv_values, preferred_element_type=jnp.float32
    ).astype(jnp.bfloat16)[None, None]
    return (hidden, page_keys, page_values)


def solution(mesh):
    placed = (
        P(("grp", "row"), None, "col"),
        P(None, "col"),
        P(None, "col"),
        P(None, "col"),
        P("col", None),
        P(),
        P(("grp", "row"), None, None, "col"),
        P(("grp", "row"), None, None, "col"),
        P(("grp", "row")),
        P(("grp", "row")),
        P(("grp", "row"), None),
        P(),
    )
    return jax.shard_map(
        local,
        mesh=mesh,
        in_specs=placed,
        out_specs=(
            P(("grp", "row"), None, "col"),
            P("grp", "row", None, None, "col"),
            P("grp", "row", None, None, "col"),
        ),
        check_vma=False,
    )
```

```python
import functools
import jax
import jax.numpy as jnp
from jax import lax
from jax.experimental import pallas as pl
from jax.experimental.pallas import tpu as pltpu
from jax.sharding import PartitionSpec as P

D = 2048
DK = 128
DV = 256


EPS_INPUT = 1e-06
EPS_HEAD = 1e-05
OUT_SCALE = 0.8


def swapped(x, axis, stride):
    return lax.ppermute(x, axis, [(i, i ^ 1 << stride) for i in range(lax.axis_size(axis))])


def head_attend(queries_in, key_set, value_set, allowed):
    scores = jnp.einsum(
        "chd,khd->hck", queries_in, key_set, preferred_element_type=jnp.float32
    ) * queries_in.shape[-1] ** (-0.5)
    scores = jnp.where(allowed[None], scores, -jnp.inf)
    highest = jnp.max(scores, axis=-1, keepdims=True)
    exp_scores = jnp.exp(scores - highest)
    weights = (exp_scores / jnp.sum(exp_scores, axis=-1, keepdims=True)).astype(jnp.bfloat16)
    return jnp.einsum("hck,khe->che", weights, value_set, preferred_element_type=jnp.float32)


def arrange(is_first, own_part, other_part):
    return (jnp.where(is_first, own_part, other_part), jnp.where(is_first, other_part, own_part))


def head_norm(differ):
    return (
        OUT_SCALE * differ * lax.rsqrt(jnp.mean(differ * differ, axis=-1, keepdims=True) + EPS_HEAD)
    )


MASKED = -1e30
LOG2E = 1.4426950408889634


def fits_kernel(w_query, prefix_keys):
    return w_query.shape[1] % (2 * DK) == 0 and lax.axis_size("grp") == 4


def kernel(
    n_col,
    n_row,
    new_len,
    prefix_len,
    holder,
    page_table,
    diff_lambda,
    tokens,
    w_query,
    w_key,
    w_value,
    w_out,
    prefix_keys,
    prefix_values,
    hidden,
    page_keys,
    page_values,
    tok,
    weights,
    w_last,
    kbuf,
    vbuf,
    sums,
    queries,
    acc,
    top,
    low,
    attended,
    outgoing,
    incoming,
    page_out,
    page_in,
    local_sem,
    tok_send,
    tok_recv,
    pre_send,
    pre_recv,
    page_send,
    page_recv,
    mix_send,
    mix_recv,
):
    groups = 4
    grp = lax.axis_index("grp")
    row = lax.axis_index("row")
    col = lax.axis_index("col")
    slots, cols = tok.shape[1], tok.shape[2]
    heads = queries.shape[1] // (2 * DK)
    block = kbuf.shape[1]
    page = slots // groups
    peers = (None, grp + 1 - 2 * lax.rem(grp, 2), lax.rem(grp + 2, groups), groups - 1 - grp)

    def ahead(step):
        return lax.rem(col + step, n_col)

    def behind(step):
        return lax.rem(col + n_col - step, n_col)

    copies = [
        pltpu.make_async_copy(tokens.at[0], tok.at[0], local_sem.at[0]),
        pltpu.make_async_copy(w_query, weights.at[0], local_sem.at[1]),
        pltpu.make_async_copy(w_key, weights.at[1], local_sem.at[2]),
        pltpu.make_async_copy(w_value, weights.at[2], local_sem.at[3]),
        pltpu.make_async_copy(prefix_keys.at[0, grp], kbuf.at[0], local_sem.at[4]),
        pltpu.make_async_copy(prefix_values.at[0, grp], vbuf.at[0], local_sem.at[5]),
        pltpu.make_async_copy(w_out, w_last, local_sem.at[6]),
    ]
    barrier = pltpu.get_barrier_semaphore()
    for step in range(1, n_col):
        pl.semaphore_signal(
            barrier, inc=1, device_id={"col": ahead(step)}, device_id_type=pl.DeviceIdType.MESH
        )
    for step in range(1, groups):
        pl.semaphore_signal(
            barrier, inc=1, device_id={"grp": peers[step]}, device_id_type=pl.DeviceIdType.MESH
        )
    for copy in copies:
        copy.start()
    pl.semaphore_wait(barrier, n_col - 1 + groups - 1)

    def remote(source, target, send, recv, where):
        return pltpu.make_async_remote_copy(
            src_ref=source,
            dst_ref=target,
            send_sem=send,
            recv_sem=recv,
            device_id=where,
            device_id_type=pl.DeviceIdType.MESH,
        )

    token_copies = [None] + [
        remote(tokens.at[0], tok.at[step], tok_send.at[step], tok_recv.at[step], {"col": ahead(step)})
        for step in range(1, n_col)
    ]
    for step in range(1, n_col):
        token_copies[step].start()
    key_copies, value_copies = [None], [None]
    for step in range(1, groups):
        peer = peers[step]
        key_copies.append(
            remote(
                prefix_keys.at[0, peer], kbuf.at[step], pre_send.at[0, step], pre_recv.at[0, step], {"grp": peer}
            )
        )
        value_copies.append(
            remote(
                prefix_values.at[0, peer], vbuf.at[step], pre_send.at[1, step], pre_recv.at[1, step], {"grp": peer}
            )
        )
    for step in (2, 3, 1):
        key_copies[step].start()
        value_copies[step].start()

    for copy in copies[:4]:
        copy.wait()
    square = jnp.zeros((slots, 1), jnp.float32)
    for step in range(n_col):
        if step:
            token_copies[step].wait_recv()
        shard = tok[step]
        as_float = shard.astype(jnp.float32)
        square = square + jnp.sum(as_float * as_float, axis=1, keepdims=True)
        first = pl.multiple_of(behind(step) * cols, cols)
        for which in range(3):
            part = jnp.dot(
                shard, weights[which, pl.ds(first, cols), :], preferred_element_type=jnp.float32
            )
            if step:
                part = part + sums[which]
            sums[which] = part
    inv_rms = lax.rsqrt(square / D + EPS_INPUT)
    live = lax.broadcasted_iota(jnp.int32, (slots, 1), 0) < new_len[0]
    queries[...] = (sums[0] * inv_rms).astype(jnp.bfloat16)
    new_keys = (sums[1] * inv_rms).astype(jnp.bfloat16)
    new_values = (sums[2] * inv_rms).astype(jnp.bfloat16)
    kbuf[groups] = new_keys
    vbuf[groups] = new_values
    page_out[0] = jnp.where(live, new_keys, jnp.zeros_like(new_keys))
    page_out[1] = jnp.where(live, new_values, jnp.zeros_like(new_values))

    scale = DK**-0.5 * LOG2E
    key_at = lax.broadcasted_iota(jnp.int32, (slots, block), 1)
    query_at = lax.broadcasted_iota(jnp.int32, (slots, block), 0)

    every = pl.ds(0, slots)
    parts = 2
    tall = slots // parts
    ranges = [pl.ds(part * tall, tall) for part in range(parts)]

    def attend(index, allowed, first, rows):
        for at in range(2 * heads):
            head = at // 2
            scores = lax.dot_general(
                queries[rows, at * DK : (at + 1) * DK],
                kbuf[index, :, at * DK : (at + 1) * DK],
                (((1,), (1,)), ((), ())),
                preferred_element_type=jnp.float32,
            )
            scores = jnp.where(allowed, scores * scale, MASKED)
            highest = jnp.max(scores, axis=1, keepdims=True)
            if not first:
                before = top[at, rows]
                highest = jnp.maximum(before, highest)
            weight = jnp.exp2(scores - highest)
            total = jnp.sum(weight, axis=1, keepdims=True)
            mixed = jnp.dot(
                weight.astype(jnp.bfloat16),
                vbuf[index, :, head * DV : (head + 1) * DV],
                preferred_element_type=jnp.float32,
            )
            if not first:
                decay = jnp.exp2(before - highest)
                total = total + low[at, rows] * decay
                mixed = mixed + acc[at, rows] * decay
            top[at, rows] = highest
            low[at, rows] = total
            acc[at, rows] = mixed

    def share(step, rows):
        first = pl.multiple_of(ahead(step) * cols, cols)
        return jnp.dot(attended[rows, :], w_last[:, pl.ds(first, cols)], preferred_element_type=jnp.float32)

    def valid(step):
        source = peers[step] if step else grp
        place = jnp.int32(0)
        for at in range(groups):
            place = jnp.where(holder[0, at] == source, at, place)
        return prefix_len[0] - place * block

    attend(groups, key_at <= query_at, True, every)
    copies[4].wait()
    copies[5].wait()
    attend(0, key_at < valid(0), False, every)
    for step in range(1, groups - 1):
        key_copies[step].wait_recv()
        value_copies[step].wait_recv()
        attend(step, key_at < valid(step), False, every)
    last = groups - 1
    key_copies[last].wait_recv()
    value_copies[last].wait_recv()
    copies[6].wait()
    key_in_part = lax.broadcasted_iota(jnp.int32, (tall, block), 1)

    mix_copies = []
    for part in range(parts):
        rows = ranges[part]
        attend(last, key_in_part < valid(last), False, rows)
        for head in range(heads):
            zero, one = 2 * head, 2 * head + 1
            differ = acc[zero, rows] * (1.0 / low[zero, rows]) - acc[one, rows] * (
                diff_lambda[col * heads + head] / low[one, rows]
            )
            normed = OUT_SCALE * differ * lax.rsqrt(jnp.mean(differ * differ, axis=1, keepdims=True) + EPS_HEAD)
            attended[rows, head * DV : (head + 1) * DV] = normed.astype(jnp.bfloat16)
        for step in range(n_col - 1, 0, -1):
            outgoing[step, rows] = share(step, rows).astype(jnp.bfloat16)
            copy = remote(
                outgoing.at[step, rows],
                incoming.at[step, rows],
                mix_send.at[step, part],
                mix_recv.at[step, part],
                {"col": ahead(step)},
            )
            copy.start()
            mix_copies.append((part, step, copy))

    page_copies = []
    for step in range(1, groups):
        peer = peers[step]
        rows = pl.ds(pl.multiple_of(peer * page, page), page)
        for kind in range(2):
            copy = remote(
                page_out.at[kind, rows],
                page_in.at[kind, grp],
                page_send.at[kind, step],
                page_recv.at[kind, step],
                {"grp": peer},
            )
            copy.start()
            page_copies.append(copy)
    for kind in range(2):
        page_in[kind, grp] = page_out[kind, pl.ds(pl.multiple_of(grp * page, page), page), :]

    for copy in page_copies:
        copy.wait_recv()
    for slot in range(groups):
        source = jnp.int32(0)
        for at in range(groups):
            source = jnp.where(page_table[grp, at * n_row + row] == slot, at, source)
        page_keys[0, 0, slot] = page_in[0, source]
        page_values[0, 0, slot] = page_in[1, source]
    for part in range(parts):
        rows = ranges[part]
        total = share(0, rows) + tok[0, rows].astype(jnp.float32)
        for where, step, copy in mix_copies:
            if where == part:
                copy.wait_recv()
                total = total + incoming[step, rows].astype(jnp.float32)
        at = lax.broadcasted_iota(jnp.int32, (tall, 1), 0) + part * tall
        hidden[0, rows] = jnp.where(at < new_len[0], total, 0.0).astype(jnp.bfloat16)
    for copy in token_copies[1:] + key_copies[1:] + value_copies[1:] + page_copies + [copy for _, _, copy in mix_copies]:
        copy.wait_send()


def fused(
    tokens,
    w_query,
    w_key,
    w_value,
    w_out,
    diff_lambda,
    prefix_keys,
    prefix_values,
    new_len,
    prefix_len,
    holder,
    page_table,
):
    n_col, n_row, groups = lax.axis_size("col"), lax.axis_size("row"), lax.axis_size("grp")
    slots, cols = tokens.shape[1:]
    depth, wide = w_query.shape
    block = prefix_keys.shape[2]
    page = slots // groups
    maps = wide // DK
    scalars = pl.BlockSpec(memory_space=pltpu.SMEM)
    remains = pl.BlockSpec(memory_space=pltpu.HBM)
    whole = pl.BlockSpec(memory_space=pltpu.VMEM)
    half, full = jnp.bfloat16, jnp.float32
    return pl.pallas_call(
        functools.partial(kernel, n_col, n_row),
        out_shape=(
            jax.ShapeDtypeStruct((1, slots, cols), half),
            jax.ShapeDtypeStruct((1, 1, groups, page, wide), half),
            jax.ShapeDtypeStruct((1, 1, groups, page, wide), half),
        ),
        in_specs=[scalars] * 5 + [remains] * 7,
        out_specs=(whole, whole, whole),
        scratch_shapes=[
            pltpu.VMEM((n_col, slots, cols), half),
            pltpu.VMEM((3, depth, wide), half),
            pltpu.VMEM(w_out.shape, half),
            pltpu.VMEM((groups + 1, block, wide), half),
            pltpu.VMEM((groups + 1, block, wide), half),
            pltpu.VMEM((3, slots, wide), full),
            pltpu.VMEM((slots, wide), half),
            pltpu.VMEM((maps, slots, DV), full),
            pltpu.VMEM((maps, slots, 1), full),
            pltpu.VMEM((maps, slots, 1), full),
            pltpu.VMEM((slots, wide), half),
            pltpu.VMEM((n_col, slots, cols), half),
            pltpu.VMEM((n_col, slots, cols), half),
            pltpu.VMEM((2, slots, wide), half),
            pltpu.VMEM((2, groups, page, wide), half),
            pltpu.SemaphoreType.DMA((7,)),
            pltpu.SemaphoreType.DMA((n_col,)),
            pltpu.SemaphoreType.DMA((n_col,)),
            pltpu.SemaphoreType.DMA((2, groups)),
            pltpu.SemaphoreType.DMA((2, groups)),
            pltpu.SemaphoreType.DMA((2, groups)),
            pltpu.SemaphoreType.DMA((2, groups)),
            pltpu.SemaphoreType.DMA((n_col, 2)),
            pltpu.SemaphoreType.DMA((n_col, 2)),
        ],
        compiler_params=pltpu.CompilerParams(
            collective_id=0, has_side_effects=True, vmem_limit_bytes=56 << 20
        ),
    )(
        new_len,
        prefix_len,
        holder,
        page_table.T,
        diff_lambda,
        tokens,
        w_query,
        w_key,
        w_value,
        w_out,
        prefix_keys,
        prefix_values,
    )


def local(
    tokens,
    w_query,
    w_key,
    w_value,
    w_out,
    diff_lambda,
    prefix_keys,
    prefix_values,
    new_len,
    prefix_len,
    holder,
    page_table,
):
    if fits_kernel(w_query, prefix_keys):
        return fused(
            tokens,
            w_query,
            w_key,
            w_value,
            w_out,
            diff_lambda,
            prefix_keys,
            prefix_values,
            new_len,
            prefix_len,
            holder,
            page_table,
        )
    groups = lax.axis_size("grp")
    row_count = lax.axis_size("row")
    grp_index = lax.axis_index("grp")
    row_index = lax.axis_index("row")
    col_index = lax.axis_index("col")
    local_tokens = tokens[0]
    slot_count = local_tokens.shape[0]
    query_cols = w_query.shape[1]
    value_cols = w_value.shape[1]
    group_ids = jnp.arange(groups, dtype=jnp.int32)
    got_keys, got_values = (
        lax.all_to_all(prefix_keys[0], "grp", split_axis=0, concat_axis=0, tiled=True),
        lax.all_to_all(prefix_values[0], "grp", split_axis=0, concat_axis=0, tiled=True),
    )
    shard_piece = lax.all_gather(local_tokens, "col", axis=1, tiled=True)

    def partial_product(weight):
        return jnp.dot(shard_piece, weight, preferred_element_type=jnp.float32)

    as_float = shard_piece.astype(jnp.float32)
    query_sum = partial_product(w_query)
    key_sum = partial_product(w_key)
    value_sum = partial_product(w_value)
    square_sum = jnp.sum(as_float * as_float, axis=1)
    inv_rms = lax.rsqrt(square_sum / D + EPS_INPUT)[:, None]
    queries = (query_sum * inv_rms).astype(jnp.bfloat16)
    new_keys = (key_sum * inv_rms).astype(jnp.bfloat16)
    new_values = (value_sum * inv_rms).astype(jnp.bfloat16)
    is_live = jnp.arange(slot_count) < new_len[0]
    zero_entry = jnp.zeros((), jnp.bfloat16)
    page_size = slot_count // groups
    send_keys = jnp.where(is_live[:, None], new_keys, zero_entry).reshape(
        groups, page_size, query_cols
    )
    send_values = jnp.where(is_live[:, None], new_values, zero_entry).reshape(
        groups, page_size, value_cols
    )
    recv_keys, recv_values = (
        lax.all_to_all(send_keys, "grp", split_axis=0, concat_axis=0, tiled=True),
        lax.all_to_all(send_values, "grp", split_axis=0, concat_axis=0, tiled=True),
    )
    pick_block = (holder[0][:, None] == group_ids[None, :]).astype(jnp.bfloat16)
    fetched_keys = (
        jnp.einsum("bh,hpc->bpc", pick_block, got_keys, preferred_element_type=jnp.float32)
        .astype(jnp.bfloat16)
        .reshape(-1, query_cols)
    )
    fetched_values = (
        jnp.einsum("bh,hpc->bpc", pick_block, got_values, preferred_element_type=jnp.float32)
        .astype(jnp.bfloat16)
        .reshape(-1, value_cols)
    )
    prefix_span = fetched_keys.shape[0]
    position = jnp.arange(prefix_span + slot_count)
    within = jnp.arange(slot_count)
    allowed = jnp.where(
        position[None, :] < prefix_span,
        position[None, :] < prefix_len[0],
        position[None, :] - prefix_span <= within[:, None],
    )
    key_own = jnp.concatenate([fetched_keys, new_keys], axis=0)
    value_own = jnp.concatenate([fetched_values, new_values], axis=0)
    if query_cols == DK:
        is_first = col_index % 2 == 0
        head_lam = diff_lambda[col_index // 2]
        half_width = DV // 2
        partner_query, partner_key, partner_value, partner_pkey, partner_pvalue = swapped(
            (queries, new_keys, new_values, fetched_keys, fetched_values), "col", 0
        )
        query_zero, query_one = arrange(is_first, queries, partner_query)
        key_zero, key_one = arrange(
            is_first, key_own, jnp.concatenate([partner_pkey, partner_key], axis=0)
        )
        value_low, value_high = arrange(
            is_first, value_own, jnp.concatenate([partner_pvalue, partner_value], axis=0)
        )
        value_full = jnp.concatenate([value_low, value_high], axis=1)[:, None, :]
        map_zero = head_attend(query_zero[:, None, :], key_zero[:, None, :], value_full, allowed)
        map_one = head_attend(query_one[:, None, :], key_one[:, None, :], value_full, allowed)
        normed = head_norm(map_zero - head_lam * map_one)
        attended = lax.dynamic_slice_in_dim(
            normed[:, 0, :], col_index % 2 * half_width, half_width, 1
        ).astype(jnp.bfloat16)
    else:
        local_heads = query_cols // (2 * DK)
        query_four = queries.reshape(slot_count, local_heads, 2, DK)
        key_four = key_own.reshape(-1, local_heads, 2, DK)
        value_three = value_own.reshape(-1, local_heads, DV)
        map_zero = head_attend(query_four[:, :, 0], key_four[:, :, 0], value_three, allowed)
        map_one = head_attend(query_four[:, :, 1], key_four[:, :, 1], value_three, allowed)
        head_lam = lax.dynamic_slice_in_dim(diff_lambda, col_index * local_heads, local_heads, 0)
        normed = head_norm(map_zero - head_lam[None, :, None] * map_one)
        attended = normed.reshape(slot_count, local_heads * DV).astype(jnp.bfloat16)
    mixed = lax.psum_scatter(
        lax.dot_general(
            w_out, attended, (((0,), (1,)), ((), ())), preferred_element_type=jnp.float32
        ),
        "col",
        scatter_dimension=0,
        tiled=True,
    ).T
    combined = local_tokens.astype(jnp.float32) + mixed
    hidden = jnp.where(is_live[:, None], combined, 0.0).astype(jnp.bfloat16)[None]
    sources = group_ids * row_count + row_index
    slot_of = page_table[sources, grp_index]
    placement_map = (slot_of[None, :] == group_ids[:, None]).astype(jnp.bfloat16)
    page_keys = jnp.einsum(
        "sg,gpc->spc", placement_map, recv_keys, preferred_element_type=jnp.float32
    ).astype(jnp.bfloat16)[None, None]
    page_values = jnp.einsum(
        "sg,gpc->spc", placement_map, recv_values, preferred_element_type=jnp.float32
    ).astype(jnp.bfloat16)[None, None]
    return (hidden, page_keys, page_values)


def solution(mesh):
    placed = (
        P(("grp", "row"), None, "col"),
        P(None, "col"),
        P(None, "col"),
        P(None, "col"),
        P("col", None),
        P(),
        P(("grp", "row"), None, None, "col"),
        P(("grp", "row"), None, None, "col"),
        P(("grp", "row")),
        P(("grp", "row")),
        P(("grp", "row"), None),
        P(),
    )
    return jax.shard_map(
        local,
        mesh=mesh,
        in_specs=placed,
        out_specs=(
            P(("grp", "row"), None, "col"),
            P("grp", "row", None, None, "col"),
            P("grp", "row", None, None, "col"),
        ),
        check_vma=False,
    )
```

```python
import functools
import jax
import jax.numpy as jnp
from jax import lax
from jax.experimental import pallas as pl
from jax.experimental.pallas import tpu as pltpu
from jax.sharding import PartitionSpec as P

D = 2048
DK = 128
DV = 256


EPS_INPUT = 1e-06
EPS_HEAD = 1e-05
OUT_SCALE = 0.8


def swapped(x, axis, stride):
    return lax.ppermute(x, axis, [(i, i ^ 1 << stride) for i in range(lax.axis_size(axis))])


def head_attend(queries_in, key_set, value_set, allowed):
    scores = jnp.einsum(
        "chd,khd->hck", queries_in, key_set, preferred_element_type=jnp.float32
    ) * queries_in.shape[-1] ** (-0.5)
    scores = jnp.where(allowed[None], scores, -jnp.inf)
    highest = jnp.max(scores, axis=-1, keepdims=True)
    exp_scores = jnp.exp(scores - highest)
    weights = (exp_scores / jnp.sum(exp_scores, axis=-1, keepdims=True)).astype(jnp.bfloat16)
    return jnp.einsum("hck,khe->che", weights, value_set, preferred_element_type=jnp.float32)


def arrange(is_first, own_part, other_part):
    return (jnp.where(is_first, own_part, other_part), jnp.where(is_first, other_part, own_part))


def head_norm(differ):
    return (
        OUT_SCALE * differ * lax.rsqrt(jnp.mean(differ * differ, axis=-1, keepdims=True) + EPS_HEAD)
    )


MASKED = -1e30
LOG2E = 1.4426950408889634


def fits_kernel(w_query, prefix_keys):
    return w_query.shape[1] % (2 * DK) == 0 and lax.axis_size("grp") == 4 and lax.axis_size("col") == 4


def kernel(
    n_col,
    n_row,
    new_len,
    prefix_len,
    holder,
    page_table,
    diff_lambda,
    tokens,
    w_query,
    w_key,
    w_value,
    w_out,
    prefix_keys,
    prefix_values,
    hidden,
    page_keys,
    page_values,
    tok,
    weights,
    w_last,
    kbuf,
    vbuf,
    sums,
    queries,
    acc,
    top,
    low,
    attended,
    outgoing,
    incoming,
    page_out,
    page_in,
    local_sem,
    tok_send,
    tok_recv,
    pre_send,
    pre_recv,
    page_send,
    page_recv,
    mix_send,
    mix_recv,
):
    groups = 4
    grp = lax.axis_index("grp")
    row = lax.axis_index("row")
    col = lax.axis_index("col")
    slots, cols = tok.shape[1], tok.shape[2]
    heads = queries.shape[1] // (2 * DK)
    block = kbuf.shape[1]
    page = slots // groups
    peers = (None, grp + 1 - 2 * lax.rem(grp, 2), lax.rem(grp + 2, groups), groups - 1 - grp)

    def ahead(step):
        return lax.rem(col + step, n_col)

    def behind(step):
        return lax.rem(col + n_col - step, n_col)

    copies = [
        pltpu.make_async_copy(tokens.at[0], tok.at[0], local_sem.at[0]),
        pltpu.make_async_copy(w_query, weights.at[0], local_sem.at[1]),
        pltpu.make_async_copy(w_key, weights.at[1], local_sem.at[2]),
        pltpu.make_async_copy(w_value, weights.at[2], local_sem.at[3]),
        pltpu.make_async_copy(prefix_keys.at[0, grp], kbuf.at[0], local_sem.at[4]),
        pltpu.make_async_copy(prefix_values.at[0, grp], vbuf.at[0], local_sem.at[5]),
        pltpu.make_async_copy(w_out, w_last, local_sem.at[6]),
    ]
    barrier = pltpu.get_barrier_semaphore()
    for step in range(1, n_col):
        pl.semaphore_signal(
            barrier, inc=1, device_id={"col": ahead(step)}, device_id_type=pl.DeviceIdType.MESH
        )
    for step in range(1, groups):
        pl.semaphore_signal(
            barrier, inc=1, device_id={"grp": peers[step]}, device_id_type=pl.DeviceIdType.MESH
        )
    for copy in copies:
        copy.start()
    pl.semaphore_wait(barrier, n_col - 1 + groups - 1)

    def remote(source, target, send, recv, where):
        return pltpu.make_async_remote_copy(
            src_ref=source,
            dst_ref=target,
            send_sem=send,
            recv_sem=recv,
            device_id=where,
            device_id_type=pl.DeviceIdType.MESH,
        )

    token_copies = [None] + [
        remote(tokens.at[0], tok.at[step], tok_send.at[step], tok_recv.at[step], {"col": ahead(step)})
        for step in range(1, n_col)
    ]
    inner = jnp.logical_and(col > 0, col < n_col - 1)
    forward_to = jnp.where(col == 1, 0, 3)
    forward_slot = jnp.where(col == 1, 1, 3)
    forward = remote(
        tok.at[2], tok.at[forward_slot], tok_send.at[0], tok_recv.at[forward_slot], {"col": forward_to}
    )
    sends_own = {1: col != 3, 2: col >= 0, 3: col != 0}
    for step in (2, 1, 3):
        pl.when(sends_own[step])(token_copies[step].start)
    key_copies, value_copies = [None], [None]
    for step in range(1, groups):
        peer = peers[step]
        key_copies.append(
            remote(
                prefix_keys.at[0, peer], kbuf.at[step], pre_send.at[0, step], pre_recv.at[0, step], {"grp": peer}
            )
        )
        value_copies.append(
            remote(
                prefix_values.at[0, peer], vbuf.at[step], pre_send.at[1, step], pre_recv.at[1, step], {"grp": peer}
            )
        )
    for step in (2, 3, 1):
        key_copies[step].start()
        value_copies[step].start()

    for copy in copies[:4]:
        copy.wait()
    square = jnp.zeros((slots, 1), jnp.float32)
    second = jnp.where(col == 0, 3, 1)
    for turn, step in enumerate((0, 2, second, 4 - second)):
        if turn:
            remote(
                tok.at[step], tok.at[step], tok_send.at[step], tok_recv.at[step], {"col": behind(step)}
            ).wait_recv()
        if turn == 1:
            pl.when(inner)(forward.start)
        shard = tok[step]
        as_float = shard.astype(jnp.float32)
        square = square + jnp.sum(as_float * as_float, axis=1, keepdims=True)
        first = pl.multiple_of(behind(step) * cols, cols)
        for which in range(3):
            part = jnp.dot(
                shard, weights[which, pl.ds(first, cols), :], preferred_element_type=jnp.float32
            )
            if turn:
                part = part + sums[which]
            sums[which] = part
    inv_rms = lax.rsqrt(square / D + EPS_INPUT)
    live = lax.broadcasted_iota(jnp.int32, (slots, 1), 0) < new_len[0]
    queries[...] = (sums[0] * inv_rms).astype(jnp.bfloat16)
    new_keys = (sums[1] * inv_rms).astype(jnp.bfloat16)
    new_values = (sums[2] * inv_rms).astype(jnp.bfloat16)
    kbuf[groups] = new_keys
    vbuf[groups] = new_values
    page_out[0] = jnp.where(live, new_keys, jnp.zeros_like(new_keys))
    page_out[1] = jnp.where(live, new_values, jnp.zeros_like(new_values))

    scale = DK**-0.5 * LOG2E
    key_at = lax.broadcasted_iota(jnp.int32, (slots, block), 1)
    query_at = lax.broadcasted_iota(jnp.int32, (slots, block), 0)

    every = pl.ds(0, slots)
    parts = 2
    tall = slots // parts
    ranges = [pl.ds(part * tall, tall) for part in range(parts)]

    def attend(index, allowed, first, rows):
        for at in range(2 * heads):
            head = at // 2
            scores = lax.dot_general(
                queries[rows, at * DK : (at + 1) * DK],
                kbuf[index, :, at * DK : (at + 1) * DK],
                (((1,), (1,)), ((), ())),
                preferred_element_type=jnp.float32,
            )
            scores = jnp.where(allowed, scores * scale, MASKED)
            highest = jnp.max(scores, axis=1, keepdims=True)
            if not first:
                before = top[at, rows]
                highest = jnp.maximum(before, highest)
            weight = jnp.exp2(scores - highest)
            total = jnp.sum(weight, axis=1, keepdims=True)
            mixed = jnp.dot(
                weight.astype(jnp.bfloat16),
                vbuf[index, :, head * DV : (head + 1) * DV],
                preferred_element_type=jnp.float32,
            )
            if not first:
                decay = jnp.exp2(before - highest)
                total = total + low[at, rows] * decay
                mixed = mixed + acc[at, rows] * decay
            top[at, rows] = highest
            low[at, rows] = total
            acc[at, rows] = mixed

    def share(step, rows):
        first = pl.multiple_of(ahead(step) * cols, cols)
        return jnp.dot(attended[rows, :], w_last[:, pl.ds(first, cols)], preferred_element_type=jnp.float32)

    def valid(step):
        source = peers[step] if step else grp
        place = jnp.int32(0)
        for at in range(groups):
            place = jnp.where(holder[0, at] == source, at, place)
        return prefix_len[0] - place * block

    attend(groups, key_at <= query_at, True, every)
    copies[4].wait()
    copies[5].wait()
    attend(0, key_at < valid(0), False, every)
    for step in range(1, groups - 1):
        key_copies[step].wait_recv()
        value_copies[step].wait_recv()
        attend(step, key_at < valid(step), False, every)
    last = groups - 1
    key_copies[last].wait_recv()
    value_copies[last].wait_recv()
    copies[6].wait()
    key_in_part = lax.broadcasted_iota(jnp.int32, (tall, block), 1)

    mix_copies = []
    for part in range(parts):
        rows = ranges[part]
        attend(last, key_in_part < valid(last), False, rows)
        for head in range(heads):
            zero, one = 2 * head, 2 * head + 1
            differ = acc[zero, rows] * (1.0 / low[zero, rows]) - acc[one, rows] * (
                diff_lambda[col * heads + head] / low[one, rows]
            )
            normed = OUT_SCALE * differ * lax.rsqrt(jnp.mean(differ * differ, axis=1, keepdims=True) + EPS_HEAD)
            attended[rows, head * DV : (head + 1) * DV] = normed.astype(jnp.bfloat16)
        for step in range(n_col - 1, 0, -1):
            outgoing[step, rows] = share(step, rows).astype(jnp.bfloat16)
            copy = remote(
                outgoing.at[step, rows],
                incoming.at[step, rows],
                mix_send.at[step, part],
                mix_recv.at[step, part],
                {"col": ahead(step)},
            )
            copy.start()
            mix_copies.append((part, step, copy))

    page_copies = []
    for step in range(1, groups):
        peer = peers[step]
        rows = pl.ds(pl.multiple_of(peer * page, page), page)
        for kind in range(2):
            copy = remote(
                page_out.at[kind, rows],
                page_in.at[kind, grp],
                page_send.at[kind, step],
                page_recv.at[kind, step],
                {"grp": peer},
            )
            copy.start()
            page_copies.append(copy)
    for kind in range(2):
        page_in[kind, grp] = page_out[kind, pl.ds(pl.multiple_of(grp * page, page), page), :]

    for copy in page_copies:
        copy.wait_recv()
    for slot in range(groups):
        source = jnp.int32(0)
        for at in range(groups):
            source = jnp.where(page_table[grp, at * n_row + row] == slot, at, source)
        page_keys[0, 0, slot] = page_in[0, source]
        page_values[0, 0, slot] = page_in[1, source]
    for part in range(parts):
        rows = ranges[part]
        total = share(0, rows) + tok[0, rows].astype(jnp.float32)
        for where, step, copy in mix_copies:
            if where == part:
                copy.wait_recv()
                total = total + incoming[step, rows].astype(jnp.float32)
        at = lax.broadcasted_iota(jnp.int32, (tall, 1), 0) + part * tall
        hidden[0, rows] = jnp.where(at < new_len[0], total, 0.0).astype(jnp.bfloat16)
    for step in range(1, n_col):
        pl.when(sends_own[step])(token_copies[step].wait_send)
    pl.when(inner)(forward.wait_send)
    for copy in key_copies[1:] + value_copies[1:] + page_copies + [copy for _, _, copy in mix_copies]:
        copy.wait_send()


def fused(
    tokens,
    w_query,
    w_key,
    w_value,
    w_out,
    diff_lambda,
    prefix_keys,
    prefix_values,
    new_len,
    prefix_len,
    holder,
    page_table,
):
    n_col, n_row, groups = lax.axis_size("col"), lax.axis_size("row"), lax.axis_size("grp")
    slots, cols = tokens.shape[1:]
    depth, wide = w_query.shape
    block = prefix_keys.shape[2]
    page = slots // groups
    maps = wide // DK
    scalars = pl.BlockSpec(memory_space=pltpu.SMEM)
    remains = pl.BlockSpec(memory_space=pltpu.HBM)
    whole = pl.BlockSpec(memory_space=pltpu.VMEM)
    half, full = jnp.bfloat16, jnp.float32
    return pl.pallas_call(
        functools.partial(kernel, n_col, n_row),
        out_shape=(
            jax.ShapeDtypeStruct((1, slots, cols), half),
            jax.ShapeDtypeStruct((1, 1, groups, page, wide), half),
            jax.ShapeDtypeStruct((1, 1, groups, page, wide), half),
        ),
        in_specs=[scalars] * 5 + [remains] * 7,
        out_specs=(whole, whole, whole),
        scratch_shapes=[
            pltpu.VMEM((n_col, slots, cols), half),
            pltpu.VMEM((3, depth, wide), half),
            pltpu.VMEM(w_out.shape, half),
            pltpu.VMEM((groups + 1, block, wide), half),
            pltpu.VMEM((groups + 1, block, wide), half),
            pltpu.VMEM((3, slots, wide), full),
            pltpu.VMEM((slots, wide), half),
            pltpu.VMEM((maps, slots, DV), full),
            pltpu.VMEM((maps, slots, 1), full),
            pltpu.VMEM((maps, slots, 1), full),
            pltpu.VMEM((slots, wide), half),
            pltpu.VMEM((n_col, slots, cols), half),
            pltpu.VMEM((n_col, slots, cols), half),
            pltpu.VMEM((2, slots, wide), half),
            pltpu.VMEM((2, groups, page, wide), half),
            pltpu.SemaphoreType.DMA((7,)),
            pltpu.SemaphoreType.DMA((n_col,)),
            pltpu.SemaphoreType.DMA((n_col,)),
            pltpu.SemaphoreType.DMA((2, groups)),
            pltpu.SemaphoreType.DMA((2, groups)),
            pltpu.SemaphoreType.DMA((2, groups)),
            pltpu.SemaphoreType.DMA((2, groups)),
            pltpu.SemaphoreType.DMA((n_col, 2)),
            pltpu.SemaphoreType.DMA((n_col, 2)),
        ],
        compiler_params=pltpu.CompilerParams(
            collective_id=0, has_side_effects=True, vmem_limit_bytes=30 << 20
        ),
    )(
        new_len,
        prefix_len,
        holder,
        page_table.T,
        diff_lambda,
        tokens,
        w_query,
        w_key,
        w_value,
        w_out,
        prefix_keys,
        prefix_values,
    )


def local(
    tokens,
    w_query,
    w_key,
    w_value,
    w_out,
    diff_lambda,
    prefix_keys,
    prefix_values,
    new_len,
    prefix_len,
    holder,
    page_table,
):
    if fits_kernel(w_query, prefix_keys):
        return fused(
            tokens,
            w_query,
            w_key,
            w_value,
            w_out,
            diff_lambda,
            prefix_keys,
            prefix_values,
            new_len,
            prefix_len,
            holder,
            page_table,
        )
    groups = lax.axis_size("grp")
    row_count = lax.axis_size("row")
    grp_index = lax.axis_index("grp")
    row_index = lax.axis_index("row")
    col_index = lax.axis_index("col")
    local_tokens = tokens[0]
    slot_count = local_tokens.shape[0]
    query_cols = w_query.shape[1]
    value_cols = w_value.shape[1]
    group_ids = jnp.arange(groups, dtype=jnp.int32)
    got_keys, got_values = (
        lax.all_to_all(prefix_keys[0], "grp", split_axis=0, concat_axis=0, tiled=True),
        lax.all_to_all(prefix_values[0], "grp", split_axis=0, concat_axis=0, tiled=True),
    )
    shard_piece = lax.all_gather(local_tokens, "col", axis=1, tiled=True)

    def partial_product(weight):
        return jnp.dot(shard_piece, weight, preferred_element_type=jnp.float32)

    as_float = shard_piece.astype(jnp.float32)
    query_sum = partial_product(w_query)
    key_sum = partial_product(w_key)
    value_sum = partial_product(w_value)
    square_sum = jnp.sum(as_float * as_float, axis=1)
    inv_rms = lax.rsqrt(square_sum / D + EPS_INPUT)[:, None]
    queries = (query_sum * inv_rms).astype(jnp.bfloat16)
    new_keys = (key_sum * inv_rms).astype(jnp.bfloat16)
    new_values = (value_sum * inv_rms).astype(jnp.bfloat16)
    is_live = jnp.arange(slot_count) < new_len[0]
    zero_entry = jnp.zeros((), jnp.bfloat16)
    page_size = slot_count // groups
    send_keys = jnp.where(is_live[:, None], new_keys, zero_entry).reshape(
        groups, page_size, query_cols
    )
    send_values = jnp.where(is_live[:, None], new_values, zero_entry).reshape(
        groups, page_size, value_cols
    )
    recv_keys, recv_values = (
        lax.all_to_all(send_keys, "grp", split_axis=0, concat_axis=0, tiled=True),
        lax.all_to_all(send_values, "grp", split_axis=0, concat_axis=0, tiled=True),
    )
    pick_block = (holder[0][:, None] == group_ids[None, :]).astype(jnp.bfloat16)
    fetched_keys = (
        jnp.einsum("bh,hpc->bpc", pick_block, got_keys, preferred_element_type=jnp.float32)
        .astype(jnp.bfloat16)
        .reshape(-1, query_cols)
    )
    fetched_values = (
        jnp.einsum("bh,hpc->bpc", pick_block, got_values, preferred_element_type=jnp.float32)
        .astype(jnp.bfloat16)
        .reshape(-1, value_cols)
    )
    prefix_span = fetched_keys.shape[0]
    position = jnp.arange(prefix_span + slot_count)
    within = jnp.arange(slot_count)
    allowed = jnp.where(
        position[None, :] < prefix_span,
        position[None, :] < prefix_len[0],
        position[None, :] - prefix_span <= within[:, None],
    )
    key_own = jnp.concatenate([fetched_keys, new_keys], axis=0)
    value_own = jnp.concatenate([fetched_values, new_values], axis=0)
    if query_cols == DK:
        is_first = col_index % 2 == 0
        head_lam = diff_lambda[col_index // 2]
        half_width = DV // 2
        partner_query, partner_key, partner_value, partner_pkey, partner_pvalue = swapped(
            (queries, new_keys, new_values, fetched_keys, fetched_values), "col", 0
        )
        query_zero, query_one = arrange(is_first, queries, partner_query)
        key_zero, key_one = arrange(
            is_first, key_own, jnp.concatenate([partner_pkey, partner_key], axis=0)
        )
        value_low, value_high = arrange(
            is_first, value_own, jnp.concatenate([partner_pvalue, partner_value], axis=0)
        )
        value_full = jnp.concatenate([value_low, value_high], axis=1)[:, None, :]
        map_zero = head_attend(query_zero[:, None, :], key_zero[:, None, :], value_full, allowed)
        map_one = head_attend(query_one[:, None, :], key_one[:, None, :], value_full, allowed)
        normed = head_norm(map_zero - head_lam * map_one)
        attended = lax.dynamic_slice_in_dim(
            normed[:, 0, :], col_index % 2 * half_width, half_width, 1
        ).astype(jnp.bfloat16)
    else:
        local_heads = query_cols // (2 * DK)
        query_four = queries.reshape(slot_count, local_heads, 2, DK)
        key_four = key_own.reshape(-1, local_heads, 2, DK)
        value_three = value_own.reshape(-1, local_heads, DV)
        map_zero = head_attend(query_four[:, :, 0], key_four[:, :, 0], value_three, allowed)
        map_one = head_attend(query_four[:, :, 1], key_four[:, :, 1], value_three, allowed)
        head_lam = lax.dynamic_slice_in_dim(diff_lambda, col_index * local_heads, local_heads, 0)
        normed = head_norm(map_zero - head_lam[None, :, None] * map_one)
        attended = normed.reshape(slot_count, local_heads * DV).astype(jnp.bfloat16)
    mixed = lax.psum_scatter(
        lax.dot_general(
            w_out, attended, (((0,), (1,)), ((), ())), preferred_element_type=jnp.float32
        ),
        "col",
        scatter_dimension=0,
        tiled=True,
    ).T
    combined = local_tokens.astype(jnp.float32) + mixed
    hidden = jnp.where(is_live[:, None], combined, 0.0).astype(jnp.bfloat16)[None]
    sources = group_ids * row_count + row_index
    slot_of = page_table[sources, grp_index]
    placement_map = (slot_of[None, :] == group_ids[:, None]).astype(jnp.bfloat16)
    page_keys = jnp.einsum(
        "sg,gpc->spc", placement_map, recv_keys, preferred_element_type=jnp.float32
    ).astype(jnp.bfloat16)[None, None]
    page_values = jnp.einsum(
        "sg,gpc->spc", placement_map, recv_values, preferred_element_type=jnp.float32
    ).astype(jnp.bfloat16)[None, None]
    return (hidden, page_keys, page_values)


def solution(mesh):
    placed = (
        P(("grp", "row"), None, "col"),
        P(None, "col"),
        P(None, "col"),
        P(None, "col"),
        P("col", None),
        P(),
        P(("grp", "row"), None, None, "col"),
        P(("grp", "row"), None, None, "col"),
        P(("grp", "row")),
        P(("grp", "row")),
        P(("grp", "row"), None),
        P(),
    )
    return jax.shard_map(
        local,
        mesh=mesh,
        in_specs=placed,
        out_specs=(
            P(("grp", "row"), None, "col"),
            P("grp", "row", None, None, "col"),
            P("grp", "row", None, None, "col"),
        ),
        check_vma=False,
    )
```

```python
import functools
import jax
import jax.numpy as jnp
from jax import lax
from jax.experimental import pallas as pl
from jax.experimental.pallas import tpu as pltpu
from jax.sharding import PartitionSpec as P

D = 2048
DK = 128
DV = 256


EPS_INPUT = 1e-06
EPS_HEAD = 1e-05
OUT_SCALE = 0.8


def swapped(x, axis, stride):
    return lax.ppermute(x, axis, [(i, i ^ 1 << stride) for i in range(lax.axis_size(axis))])


def head_attend(queries_in, key_set, value_set, allowed):
    scores = jnp.einsum(
        "chd,khd->hck", queries_in, key_set, preferred_element_type=jnp.float32
    ) * queries_in.shape[-1] ** (-0.5)
    scores = jnp.where(allowed[None], scores, -jnp.inf)
    highest = jnp.max(scores, axis=-1, keepdims=True)
    exp_scores = jnp.exp(scores - highest)
    weights = (exp_scores / jnp.sum(exp_scores, axis=-1, keepdims=True)).astype(jnp.bfloat16)
    return jnp.einsum("hck,khe->che", weights, value_set, preferred_element_type=jnp.float32)


def arrange(is_first, own_part, other_part):
    return (jnp.where(is_first, own_part, other_part), jnp.where(is_first, other_part, own_part))


def head_norm(differ):
    return (
        OUT_SCALE * differ * lax.rsqrt(jnp.mean(differ * differ, axis=-1, keepdims=True) + EPS_HEAD)
    )


MASKED = -1e30
LOG2E = 1.4426950408889634


def fits_kernel(w_query, prefix_keys):
    return w_query.shape[1] % (2 * DK) == 0 and lax.axis_size("grp") == 4 and lax.axis_size("col") == 4


def kernel(
    n_col,
    n_row,
    new_len,
    prefix_len,
    holder,
    page_table,
    diff_lambda,
    tokens,
    w_query,
    w_key,
    w_value,
    w_out,
    prefix_keys,
    prefix_values,
    hidden,
    page_keys,
    page_values,
    tok,
    weights,
    w_last,
    kbuf,
    vbuf,
    sums,
    queries,
    acc,
    top,
    low,
    attended,
    outgoing,
    incoming,
    page_out,
    page_in,
    local_sem,
    tok_send,
    tok_recv,
    pre_send,
    pre_recv,
    page_send,
    page_recv,
    mix_send,
    mix_recv,
):
    groups = 4
    grp = lax.axis_index("grp")
    row = lax.axis_index("row")
    col = lax.axis_index("col")
    slots, cols = tok.shape[1], tok.shape[2]
    heads = queries.shape[1] // (2 * DK)
    block = kbuf.shape[1]
    page = slots // groups
    peers = (None, grp + 1 - 2 * lax.rem(grp, 2), lax.rem(grp + 2, groups), groups - 1 - grp)

    def ahead(step):
        return lax.rem(col + step, n_col)

    def behind(step):
        return lax.rem(col + n_col - step, n_col)

    copies = [
        pltpu.make_async_copy(tokens.at[0], tok.at[0], local_sem.at[0]),
        pltpu.make_async_copy(w_query, weights.at[0], local_sem.at[1]),
        pltpu.make_async_copy(w_key, weights.at[1], local_sem.at[2]),
        pltpu.make_async_copy(w_value, weights.at[2], local_sem.at[3]),
        pltpu.make_async_copy(prefix_keys.at[0, grp], kbuf.at[0], local_sem.at[4]),
        pltpu.make_async_copy(prefix_values.at[0, grp], vbuf.at[0], local_sem.at[5]),
        pltpu.make_async_copy(w_out, w_last, local_sem.at[6]),
    ]
    barrier = pltpu.get_barrier_semaphore()
    for step in range(1, n_col):
        pl.semaphore_signal(
            barrier, inc=1, device_id={"col": ahead(step)}, device_id_type=pl.DeviceIdType.MESH
        )
    for step in range(1, groups):
        pl.semaphore_signal(
            barrier, inc=1, device_id={"grp": peers[step]}, device_id_type=pl.DeviceIdType.MESH
        )
    for copy in copies:
        copy.start()
    pl.semaphore_wait(barrier, n_col - 1 + groups - 1)

    def remote(source, target, send, recv, where):
        return pltpu.make_async_remote_copy(
            src_ref=source,
            dst_ref=target,
            send_sem=send,
            recv_sem=recv,
            device_id=where,
            device_id_type=pl.DeviceIdType.MESH,
        )

    token_copies = [None] + [
        remote(tokens.at[0], tok.at[step], tok_send.at[step], tok_recv.at[step], {"col": ahead(step)})
        for step in range(1, n_col)
    ]
    inner = jnp.logical_and(col > 0, col < n_col - 1)
    forward_to = jnp.where(col == 1, 0, 3)
    forward_slot = jnp.where(col == 1, 1, 3)
    forward = remote(
        tok.at[2], tok.at[forward_slot], tok_send.at[0], tok_recv.at[forward_slot], {"col": forward_to}
    )
    sends_own = {1: col != 3, 2: col >= 0, 3: col != 0}
    for step in (2, 1, 3):
        pl.when(sends_own[step])(token_copies[step].start)
    key_copies, value_copies = [None], [None]
    for step in range(1, groups):
        peer = peers[step]
        key_copies.append(
            remote(
                prefix_keys.at[0, peer], kbuf.at[step], pre_send.at[0, step], pre_recv.at[0, step], {"grp": peer}
            )
        )
        value_copies.append(
            remote(
                prefix_values.at[0, peer], vbuf.at[step], pre_send.at[1, step], pre_recv.at[1, step], {"grp": peer}
            )
        )
    for step in (2, 3, 1):
        key_copies[step].start()
        value_copies[step].start()

    for copy in copies[:4]:
        copy.wait()
    square = jnp.zeros((slots, 1), jnp.float32)
    second = jnp.where(col == 0, 3, 1)
    for turn, step in enumerate((0, 2, second, 4 - second)):
        if turn:
            remote(
                tok.at[step], tok.at[step], tok_send.at[step], tok_recv.at[step], {"col": behind(step)}
            ).wait_recv()
        if turn == 1:
            pl.when(inner)(forward.start)
        shard = tok[step]
        as_float = shard.astype(jnp.float32)
        square = square + jnp.sum(as_float * as_float, axis=1, keepdims=True)
        first = pl.multiple_of(behind(step) * cols, cols)
        for which in range(3):
            part = jnp.dot(
                shard, weights[which, pl.ds(first, cols), :], preferred_element_type=jnp.float32
            )
            if turn:
                part = part + sums[which]
            sums[which] = part
    inv_rms = lax.rsqrt(square / D + EPS_INPUT)
    live = lax.broadcasted_iota(jnp.int32, (slots, 1), 0) < new_len[0]
    queries[...] = (sums[0] * inv_rms).astype(jnp.bfloat16)
    new_keys = (sums[1] * inv_rms).astype(jnp.bfloat16)
    new_values = (sums[2] * inv_rms).astype(jnp.bfloat16)
    kbuf[groups] = new_keys
    vbuf[groups] = new_values
    page_out[0] = jnp.where(live, new_keys, jnp.zeros_like(new_keys))
    page_out[1] = jnp.where(live, new_values, jnp.zeros_like(new_values))

    scale = DK**-0.5 * LOG2E
    key_at = lax.broadcasted_iota(jnp.int32, (slots, block), 1)
    query_at = lax.broadcasted_iota(jnp.int32, (slots, block), 0)

    every = pl.ds(0, slots)
    parts = 2
    tall = slots // parts
    ranges = [pl.ds(part * tall, tall) for part in range(parts)]

    def attend(index, allowed, first, rows):
        for at in range(2 * heads):
            head = at // 2
            scores = lax.dot_general(
                queries[rows, at * DK : (at + 1) * DK],
                kbuf[index, :, at * DK : (at + 1) * DK],
                (((1,), (1,)), ((), ())),
                preferred_element_type=jnp.float32,
            )
            scores = jnp.where(allowed, scores * scale, MASKED)
            highest = jnp.max(scores, axis=1, keepdims=True)
            if not first:
                before = top[at, rows]
                highest = jnp.maximum(before, highest)
            weight = jnp.exp2(scores - highest)
            total = jnp.sum(weight, axis=1, keepdims=True)
            mixed = jnp.dot(
                weight.astype(jnp.bfloat16),
                vbuf[index, :, head * DV : (head + 1) * DV],
                preferred_element_type=jnp.float32,
            )
            if not first:
                decay = jnp.exp2(before - highest)
                total = total + low[at, rows] * decay
                mixed = mixed + acc[at, rows] * decay
            top[at, rows] = highest
            low[at, rows] = total
            acc[at, rows] = mixed

    def share(step, rows):
        first = pl.multiple_of(ahead(step) * cols, cols)
        return jnp.dot(attended[rows, :], w_last[:, pl.ds(first, cols)], preferred_element_type=jnp.float32)

    def valid(step):
        source = peers[step] if step else grp
        place = jnp.int32(0)
        for at in range(groups):
            place = jnp.where(holder[0, at] == source, at, place)
        return prefix_len[0] - place * block

    attend(groups, key_at <= query_at, True, every)
    copies[4].wait()
    copies[5].wait()
    attend(0, key_at < valid(0), False, every)
    for step in range(1, groups - 1):
        key_copies[step].wait_recv()
        value_copies[step].wait_recv()
        attend(step, key_at < valid(step), False, every)
    last = groups - 1
    key_copies[last].wait_recv()
    value_copies[last].wait_recv()
    copies[6].wait()
    key_in_part = lax.broadcasted_iota(jnp.int32, (tall, block), 1)

    crossing = 3 - 2 * lax.rem(col, 2)
    mix_copies = []
    for part in range(parts):
        rows = ranges[part]
        attend(last, key_in_part < valid(last), False, rows)
        for head in range(heads):
            zero, one = 2 * head, 2 * head + 1
            differ = acc[zero, rows] * (1.0 / low[zero, rows]) - acc[one, rows] * (
                diff_lambda[col * heads + head] / low[one, rows]
            )
            normed = OUT_SCALE * differ * lax.rsqrt(jnp.mean(differ * differ, axis=1, keepdims=True) + EPS_HEAD)
            attended[rows, head * DV : (head + 1) * DV] = normed.astype(jnp.bfloat16)
        for step in (2, crossing, 4 - crossing):
            outgoing[step, rows] = share(step, rows).astype(jnp.bfloat16)
            copy = remote(
                outgoing.at[step, rows],
                incoming.at[step, rows],
                mix_send.at[step, part],
                mix_recv.at[step, part],
                {"col": ahead(step)},
            )
            copy.start()
            mix_copies.append((part, step, copy))

    page_copies = []
    for step in range(1, groups):
        peer = peers[step]
        rows = pl.ds(pl.multiple_of(peer * page, page), page)
        for kind in range(2):
            copy = remote(
                page_out.at[kind, rows],
                page_in.at[kind, grp],
                page_send.at[kind, step],
                page_recv.at[kind, step],
                {"grp": peer},
            )
            copy.start()
            page_copies.append(copy)
    for kind in range(2):
        page_in[kind, grp] = page_out[kind, pl.ds(pl.multiple_of(grp * page, page), page), :]

    for copy in page_copies:
        copy.wait_recv()
    for slot in range(groups):
        source = jnp.int32(0)
        for at in range(groups):
            source = jnp.where(page_table[grp, at * n_row + row] == slot, at, source)
        page_keys[0, 0, slot] = page_in[0, source]
        page_values[0, 0, slot] = page_in[1, source]
    for part in range(parts):
        rows = ranges[part]
        total = share(0, rows) + tok[0, rows].astype(jnp.float32)
        for where, step, copy in mix_copies:
            if where == part:
                copy.wait_recv()
                total = total + incoming[step, rows].astype(jnp.float32)
        at = lax.broadcasted_iota(jnp.int32, (tall, 1), 0) + part * tall
        hidden[0, rows] = jnp.where(at < new_len[0], total, 0.0).astype(jnp.bfloat16)
    for step in range(1, n_col):
        pl.when(sends_own[step])(token_copies[step].wait_send)
    pl.when(inner)(forward.wait_send)
    for copy in key_copies[1:] + value_copies[1:] + page_copies + [copy for _, _, copy in mix_copies]:
        copy.wait_send()


def fused(
    tokens,
    w_query,
    w_key,
    w_value,
    w_out,
    diff_lambda,
    prefix_keys,
    prefix_values,
    new_len,
    prefix_len,
    holder,
    page_table,
):
    n_col, n_row, groups = lax.axis_size("col"), lax.axis_size("row"), lax.axis_size("grp")
    slots, cols = tokens.shape[1:]
    depth, wide = w_query.shape
    block = prefix_keys.shape[2]
    page = slots // groups
    maps = wide // DK
    scalars = pl.BlockSpec(memory_space=pltpu.SMEM)
    remains = pl.BlockSpec(memory_space=pltpu.HBM)
    whole = pl.BlockSpec(memory_space=pltpu.VMEM)
    half, full = jnp.bfloat16, jnp.float32
    return pl.pallas_call(
        functools.partial(kernel, n_col, n_row),
        out_shape=(
            jax.ShapeDtypeStruct((1, slots, cols), half),
            jax.ShapeDtypeStruct((1, 1, groups, page, wide), half),
            jax.ShapeDtypeStruct((1, 1, groups, page, wide), half),
        ),
        in_specs=[scalars] * 5 + [remains] * 7,
        out_specs=(whole, whole, whole),
        scratch_shapes=[
            pltpu.VMEM((n_col, slots, cols), half),
            pltpu.VMEM((3, depth, wide), half),
            pltpu.VMEM(w_out.shape, half),
            pltpu.VMEM((groups + 1, block, wide), half),
            pltpu.VMEM((groups + 1, block, wide), half),
            pltpu.VMEM((3, slots, wide), full),
            pltpu.VMEM((slots, wide), half),
            pltpu.VMEM((maps, slots, DV), full),
            pltpu.VMEM((maps, slots, 1), full),
            pltpu.VMEM((maps, slots, 1), full),
            pltpu.VMEM((slots, wide), half),
            pltpu.VMEM((n_col, slots, cols), half),
            pltpu.VMEM((n_col, slots, cols), half),
            pltpu.VMEM((2, slots, wide), half),
            pltpu.VMEM((2, groups, page, wide), half),
            pltpu.SemaphoreType.DMA((7,)),
            pltpu.SemaphoreType.DMA((n_col,)),
            pltpu.SemaphoreType.DMA((n_col,)),
            pltpu.SemaphoreType.DMA((2, groups)),
            pltpu.SemaphoreType.DMA((2, groups)),
            pltpu.SemaphoreType.DMA((2, groups)),
            pltpu.SemaphoreType.DMA((2, groups)),
            pltpu.SemaphoreType.DMA((n_col, 2)),
            pltpu.SemaphoreType.DMA((n_col, 2)),
        ],
        compiler_params=pltpu.CompilerParams(
            collective_id=0, has_side_effects=True, vmem_limit_bytes=56 << 20
        ),
    )(
        new_len,
        prefix_len,
        holder,
        page_table.T,
        diff_lambda,
        tokens,
        w_query,
        w_key,
        w_value,
        w_out,
        prefix_keys,
        prefix_values,
    )


def local(
    tokens,
    w_query,
    w_key,
    w_value,
    w_out,
    diff_lambda,
    prefix_keys,
    prefix_values,
    new_len,
    prefix_len,
    holder,
    page_table,
):
    if fits_kernel(w_query, prefix_keys):
        return fused(
            tokens,
            w_query,
            w_key,
            w_value,
            w_out,
            diff_lambda,
            prefix_keys,
            prefix_values,
            new_len,
            prefix_len,
            holder,
            page_table,
        )
    groups = lax.axis_size("grp")
    row_count = lax.axis_size("row")
    grp_index = lax.axis_index("grp")
    row_index = lax.axis_index("row")
    col_index = lax.axis_index("col")
    local_tokens = tokens[0]
    slot_count = local_tokens.shape[0]
    query_cols = w_query.shape[1]
    value_cols = w_value.shape[1]
    group_ids = jnp.arange(groups, dtype=jnp.int32)
    got_keys, got_values = (
        lax.all_to_all(prefix_keys[0], "grp", split_axis=0, concat_axis=0, tiled=True),
        lax.all_to_all(prefix_values[0], "grp", split_axis=0, concat_axis=0, tiled=True),
    )
    shard_piece = lax.all_gather(local_tokens, "col", axis=1, tiled=True)

    def partial_product(weight):
        return jnp.dot(shard_piece, weight, preferred_element_type=jnp.float32)

    as_float = shard_piece.astype(jnp.float32)
    query_sum = partial_product(w_query)
    key_sum = partial_product(w_key)
    value_sum = partial_product(w_value)
    square_sum = jnp.sum(as_float * as_float, axis=1)
    inv_rms = lax.rsqrt(square_sum / D + EPS_INPUT)[:, None]
    queries = (query_sum * inv_rms).astype(jnp.bfloat16)
    new_keys = (key_sum * inv_rms).astype(jnp.bfloat16)
    new_values = (value_sum * inv_rms).astype(jnp.bfloat16)
    is_live = jnp.arange(slot_count) < new_len[0]
    zero_entry = jnp.zeros((), jnp.bfloat16)
    page_size = slot_count // groups
    send_keys = jnp.where(is_live[:, None], new_keys, zero_entry).reshape(
        groups, page_size, query_cols
    )
    send_values = jnp.where(is_live[:, None], new_values, zero_entry).reshape(
        groups, page_size, value_cols
    )
    recv_keys, recv_values = (
        lax.all_to_all(send_keys, "grp", split_axis=0, concat_axis=0, tiled=True),
        lax.all_to_all(send_values, "grp", split_axis=0, concat_axis=0, tiled=True),
    )
    pick_block = (holder[0][:, None] == group_ids[None, :]).astype(jnp.bfloat16)
    fetched_keys = (
        jnp.einsum("bh,hpc->bpc", pick_block, got_keys, preferred_element_type=jnp.float32)
        .astype(jnp.bfloat16)
        .reshape(-1, query_cols)
    )
    fetched_values = (
        jnp.einsum("bh,hpc->bpc", pick_block, got_values, preferred_element_type=jnp.float32)
        .astype(jnp.bfloat16)
        .reshape(-1, value_cols)
    )
    prefix_span = fetched_keys.shape[0]
    position = jnp.arange(prefix_span + slot_count)
    within = jnp.arange(slot_count)
    allowed = jnp.where(
        position[None, :] < prefix_span,
        position[None, :] < prefix_len[0],
        position[None, :] - prefix_span <= within[:, None],
    )
    key_own = jnp.concatenate([fetched_keys, new_keys], axis=0)
    value_own = jnp.concatenate([fetched_values, new_values], axis=0)
    if query_cols == DK:
        is_first = col_index % 2 == 0
        head_lam = diff_lambda[col_index // 2]
        half_width = DV // 2
        partner_query, partner_key, partner_value, partner_pkey, partner_pvalue = swapped(
            (queries, new_keys, new_values, fetched_keys, fetched_values), "col", 0
        )
        query_zero, query_one = arrange(is_first, queries, partner_query)
        key_zero, key_one = arrange(
            is_first, key_own, jnp.concatenate([partner_pkey, partner_key], axis=0)
        )
        value_low, value_high = arrange(
            is_first, value_own, jnp.concatenate([partner_pvalue, partner_value], axis=0)
        )
        value_full = jnp.concatenate([value_low, value_high], axis=1)[:, None, :]
        map_zero = head_attend(query_zero[:, None, :], key_zero[:, None, :], value_full, allowed)
        map_one = head_attend(query_one[:, None, :], key_one[:, None, :], value_full, allowed)
        normed = head_norm(map_zero - head_lam * map_one)
        attended = lax.dynamic_slice_in_dim(
            normed[:, 0, :], col_index % 2 * half_width, half_width, 1
        ).astype(jnp.bfloat16)
    else:
        local_heads = query_cols // (2 * DK)
        query_four = queries.reshape(slot_count, local_heads, 2, DK)
        key_four = key_own.reshape(-1, local_heads, 2, DK)
        value_three = value_own.reshape(-1, local_heads, DV)
        map_zero = head_attend(query_four[:, :, 0], key_four[:, :, 0], value_three, allowed)
        map_one = head_attend(query_four[:, :, 1], key_four[:, :, 1], value_three, allowed)
        head_lam = lax.dynamic_slice_in_dim(diff_lambda, col_index * local_heads, local_heads, 0)
        normed = head_norm(map_zero - head_lam[None, :, None] * map_one)
        attended = normed.reshape(slot_count, local_heads * DV).astype(jnp.bfloat16)
    mixed = lax.psum_scatter(
        lax.dot_general(
            w_out, attended, (((0,), (1,)), ((), ())), preferred_element_type=jnp.float32
        ),
        "col",
        scatter_dimension=0,
        tiled=True,
    ).T
    combined = local_tokens.astype(jnp.float32) + mixed
    hidden = jnp.where(is_live[:, None], combined, 0.0).astype(jnp.bfloat16)[None]
    sources = group_ids * row_count + row_index
    slot_of = page_table[sources, grp_index]
    placement_map = (slot_of[None, :] == group_ids[:, None]).astype(jnp.bfloat16)
    page_keys = jnp.einsum(
        "sg,gpc->spc", placement_map, recv_keys, preferred_element_type=jnp.float32
    ).astype(jnp.bfloat16)[None, None]
    page_values = jnp.einsum(
        "sg,gpc->spc", placement_map, recv_values, preferred_element_type=jnp.float32
    ).astype(jnp.bfloat16)[None, None]
    return (hidden, page_keys, page_values)


def solution(mesh):
    placed = (
        P(("grp", "row"), None, "col"),
        P(None, "col"),
        P(None, "col"),
        P(None, "col"),
        P("col", None),
        P(),
        P(("grp", "row"), None, None, "col"),
        P(("grp", "row"), None, None, "col"),
        P(("grp", "row")),
        P(("grp", "row")),
        P(("grp", "row"), None),
        P(),
    )
    return jax.shard_map(
        local,
        mesh=mesh,
        in_specs=placed,
        out_specs=(
            P(("grp", "row"), None, "col"),
            P("grp", "row", None, None, "col"),
            P("grp", "row", None, None, "col"),
        ),
        check_vma=False,
    )
```

```python
import functools
import jax
import jax.numpy as jnp
from jax import lax
from jax.experimental import pallas as pl
from jax.experimental.pallas import tpu as pltpu
from jax.sharding import PartitionSpec as P

D = 2048
DK = 128
DV = 256


EPS_INPUT = 1e-06
EPS_HEAD = 1e-05
OUT_SCALE = 0.8


def swapped(x, axis, stride):
    return lax.ppermute(x, axis, [(i, i ^ 1 << stride) for i in range(lax.axis_size(axis))])


def head_attend(queries_in, key_set, value_set, allowed):
    scores = jnp.einsum(
        "chd,khd->hck", queries_in, key_set, preferred_element_type=jnp.float32
    ) * queries_in.shape[-1] ** (-0.5)
    scores = jnp.where(allowed[None], scores, -jnp.inf)
    highest = jnp.max(scores, axis=-1, keepdims=True)
    exp_scores = jnp.exp(scores - highest)
    weights = (exp_scores / jnp.sum(exp_scores, axis=-1, keepdims=True)).astype(jnp.bfloat16)
    return jnp.einsum("hck,khe->che", weights, value_set, preferred_element_type=jnp.float32)


def arrange(is_first, own_part, other_part):
    return (jnp.where(is_first, own_part, other_part), jnp.where(is_first, other_part, own_part))


def head_norm(differ):
    return (
        OUT_SCALE * differ * lax.rsqrt(jnp.mean(differ * differ, axis=-1, keepdims=True) + EPS_HEAD)
    )


MASKED = -1e30
LOG2E = 1.4426950408889634


def fits_kernel(w_query, prefix_keys):
    return w_query.shape[1] % (2 * DK) == 0 and lax.axis_size("grp") == 4 and lax.axis_size("col") == 4


def kernel(
    n_col,
    n_row,
    new_len,
    prefix_len,
    holder,
    page_table,
    diff_lambda,
    tokens,
    w_query,
    w_key,
    w_value,
    w_out,
    prefix_keys,
    prefix_values,
    hidden,
    page_keys,
    page_values,
    tok,
    weights,
    w_last,
    kbuf,
    vbuf,
    sums,
    queries,
    acc,
    top,
    low,
    attended,
    outgoing,
    incoming,
    page_out,
    page_in,
    local_sem,
    tok_send,
    tok_recv,
    pre_send,
    pre_recv,
    page_send,
    page_recv,
    mix_send,
    mix_recv,
):
    groups = 4
    grp = lax.axis_index("grp")
    row = lax.axis_index("row")
    col = lax.axis_index("col")
    slots, cols = tok.shape[1], tok.shape[2]
    heads = queries.shape[1] // (2 * DK)
    block = kbuf.shape[1]
    page = slots // groups
    peers = (None, grp + 1 - 2 * lax.rem(grp, 2), lax.rem(grp + 2, groups), groups - 1 - grp)

    def ahead(step):
        return lax.rem(col + step, n_col)

    def behind(step):
        return lax.rem(col + n_col - step, n_col)

    copies = [
        pltpu.make_async_copy(tokens.at[0], tok.at[0], local_sem.at[0]),
        pltpu.make_async_copy(w_query, weights.at[0], local_sem.at[1]),
        pltpu.make_async_copy(w_key, weights.at[1], local_sem.at[2]),
        pltpu.make_async_copy(w_value, weights.at[2], local_sem.at[3]),
        pltpu.make_async_copy(prefix_keys.at[0, grp], kbuf.at[0], local_sem.at[4]),
        pltpu.make_async_copy(prefix_values.at[0, grp], vbuf.at[0], local_sem.at[5]),
        pltpu.make_async_copy(w_out, w_last, local_sem.at[6]),
    ]
    barrier = pltpu.get_barrier_semaphore()
    for step in range(1, n_col):
        pl.semaphore_signal(
            barrier, inc=1, device_id={"col": ahead(step)}, device_id_type=pl.DeviceIdType.MESH
        )
    for step in range(1, groups):
        pl.semaphore_signal(
            barrier, inc=1, device_id={"grp": peers[step]}, device_id_type=pl.DeviceIdType.MESH
        )
    for copy in copies:
        copy.start()
    pl.semaphore_wait(barrier, n_col - 1 + groups - 1)

    def remote(source, target, send, recv, where):
        return pltpu.make_async_remote_copy(
            src_ref=source,
            dst_ref=target,
            send_sem=send,
            recv_sem=recv,
            device_id=where,
            device_id_type=pl.DeviceIdType.MESH,
        )

    token_copies = [None] + [
        remote(tokens.at[0], tok.at[step], tok_send.at[step], tok_recv.at[step], {"col": ahead(step)})
        for step in range(1, n_col)
    ]
    inner = jnp.logical_and(col > 0, col < n_col - 1)
    forward_to = jnp.where(col == 1, 0, 3)
    forward_slot = jnp.where(col == 1, 1, 3)
    forward = remote(
        tok.at[2], tok.at[forward_slot], tok_send.at[0], tok_recv.at[forward_slot], {"col": forward_to}
    )
    sends_own = {1: col != 3, 2: col >= 0, 3: col != 0}
    for step in (2, 1, 3):
        pl.when(sends_own[step])(token_copies[step].start)
    key_copies, value_copies = [None], [None]
    for step in range(1, groups):
        peer = peers[step]
        key_copies.append(
            remote(
                prefix_keys.at[0, peer], kbuf.at[step], pre_send.at[0, step], pre_recv.at[0, step], {"grp": peer}
            )
        )
        value_copies.append(
            remote(
                prefix_values.at[0, peer], vbuf.at[step], pre_send.at[1, step], pre_recv.at[1, step], {"grp": peer}
            )
        )
    for step in (2, 3, 1):
        key_copies[step].start()
        value_copies[step].start()

    for copy in copies[:4]:
        copy.wait()
    square = jnp.zeros((slots, 1), jnp.float32)
    second = jnp.where(col == 0, 3, 1)
    for turn, step in enumerate((0, 2, second, 4 - second)):
        if turn:
            remote(
                tok.at[step], tok.at[step], tok_send.at[step], tok_recv.at[step], {"col": behind(step)}
            ).wait_recv()
        if turn == 1:
            pl.when(inner)(forward.start)
        shard = tok[step]
        as_float = shard.astype(jnp.float32)
        square = square + jnp.sum(as_float * as_float, axis=1, keepdims=True)
        first = pl.multiple_of(behind(step) * cols, cols)
        for which in range(3):
            part = jnp.dot(
                shard, weights[which, pl.ds(first, cols), :], preferred_element_type=jnp.float32
            )
            if turn:
                part = part + sums[which]
            sums[which] = part
    inv_rms = lax.rsqrt(square / D + EPS_INPUT)
    live = lax.broadcasted_iota(jnp.int32, (slots, 1), 0) < new_len[0]
    queries[...] = (sums[0] * inv_rms).astype(jnp.bfloat16)
    new_keys = (sums[1] * inv_rms).astype(jnp.bfloat16)
    new_values = (sums[2] * inv_rms).astype(jnp.bfloat16)
    kbuf[groups] = new_keys
    vbuf[groups] = new_values
    page_out[0] = jnp.where(live, new_keys, jnp.zeros_like(new_keys))
    page_out[1] = jnp.where(live, new_values, jnp.zeros_like(new_values))

    scale = DK**-0.5 * LOG2E
    key_at = lax.broadcasted_iota(jnp.int32, (slots, block), 1)
    query_at = lax.broadcasted_iota(jnp.int32, (slots, block), 0)

    every = pl.ds(0, slots)
    parts = 2
    tall = slots // parts
    ranges = [pl.ds(part * tall, tall) for part in range(parts)]

    def attend(index, allowed, first, rows):
        for at in range(2 * heads):
            head = at // 2
            scores = lax.dot_general(
                queries[rows, at * DK : (at + 1) * DK],
                kbuf[index, :, at * DK : (at + 1) * DK],
                (((1,), (1,)), ((), ())),
                preferred_element_type=jnp.float32,
            )
            scores = jnp.where(allowed, scores * scale, MASKED)
            highest = jnp.max(scores, axis=1, keepdims=True)
            if not first:
                before = top[at, rows]
                highest = jnp.maximum(before, highest)
            weight = jnp.exp2(scores - highest)
            total = jnp.sum(weight, axis=1, keepdims=True)
            mixed = jnp.dot(
                weight.astype(jnp.bfloat16),
                vbuf[index, :, head * DV : (head + 1) * DV],
                preferred_element_type=jnp.float32,
            )
            if not first:
                decay = jnp.exp2(before - highest)
                total = total + low[at, rows] * decay
                mixed = mixed + acc[at, rows] * decay
            top[at, rows] = highest
            low[at, rows] = total
            acc[at, rows] = mixed

    def share(step, rows):
        first = pl.multiple_of(ahead(step) * cols, cols)
        return jnp.dot(attended[rows, :], w_last[:, pl.ds(first, cols)], preferred_element_type=jnp.float32)

    def valid(step):
        source = peers[step] if step else grp
        place = jnp.int32(0)
        for at in range(groups):
            place = jnp.where(holder[0, at] == source, at, place)
        return prefix_len[0] - place * block

    attend(groups, key_at <= query_at, True, every)
    copies[4].wait()
    copies[5].wait()
    attend(0, key_at < valid(0), False, every)
    for step in range(1, groups - 1):
        key_copies[step].wait_recv()
        value_copies[step].wait_recv()
        attend(step, key_at < valid(step), False, every)
    last = groups - 1
    key_copies[last].wait_recv()
    value_copies[last].wait_recv()
    copies[6].wait()
    key_in_part = lax.broadcasted_iota(jnp.int32, (tall, block), 1)

    crossing = 3 - 2 * lax.rem(col, 2)
    third = 4 - crossing

    def direct(part, step, slot, target):
        return remote(
            outgoing.at[step, ranges[part]],
            incoming.at[slot, ranges[part]],
            mix_send.at[step, part],
            mix_recv.at[slot, part],
            {"col": target},
        )

    def middle(part, relays):
        total = share(2, ranges[part])
        if relays:
            direct(part, 2, 0, ahead(2)).wait_recv()
            total = total + incoming[0, ranges[part]].astype(jnp.float32)
        outgoing[2, ranges[part]] = total.astype(jnp.bfloat16)
        direct(part, 2, 2, ahead(2)).start()

    @pl.when(jnp.logical_not(inner))
    def _():
        incoming[third] = jnp.zeros((slots, cols), jnp.bfloat16)

    for part in range(parts):
        rows = ranges[part]
        attend(last, key_in_part < valid(last), False, rows)
        for head in range(heads):
            zero, one = 2 * head, 2 * head + 1
            differ = acc[zero, rows] * (1.0 / low[zero, rows]) - acc[one, rows] * (
                diff_lambda[col * heads + head] / low[one, rows]
            )
            normed = OUT_SCALE * differ * lax.rsqrt(jnp.mean(differ * differ, axis=1, keepdims=True) + EPS_HEAD)
            attended[rows, head * DV : (head + 1) * DV] = normed.astype(jnp.bfloat16)
        slot = jnp.where(inner, crossing, 0)
        target = jnp.where(inner, ahead(crossing), jnp.where(col == 0, 1, 2))
        outgoing[crossing, rows] = share(crossing, rows).astype(jnp.bfloat16)
        direct(part, crossing, slot, target).start()
        pl.when(jnp.logical_not(inner))(functools.partial(middle, part, False))
        outgoing[third, rows] = share(third, rows).astype(jnp.bfloat16)
        direct(part, third, third, ahead(third)).start()
    for part in range(parts):
        pl.when(inner)(functools.partial(middle, part, True))

    page_copies = []
    for step in range(1, groups):
        peer = peers[step]
        rows = pl.ds(pl.multiple_of(peer * page, page), page)
        for kind in range(2):
            copy = remote(
                page_out.at[kind, rows],
                page_in.at[kind, grp],
                page_send.at[kind, step],
                page_recv.at[kind, step],
                {"grp": peer},
            )
            copy.start()
            page_copies.append(copy)
    for kind in range(2):
        page_in[kind, grp] = page_out[kind, pl.ds(pl.multiple_of(grp * page, page), page), :]

    for copy in page_copies:
        copy.wait_recv()
    for slot in range(groups):
        source = jnp.int32(0)
        for at in range(groups):
            source = jnp.where(page_table[grp, at * n_row + row] == slot, at, source)
        page_keys[0, 0, slot] = page_in[0, source]
        page_values[0, 0, slot] = page_in[1, source]
    for part in range(parts):
        rows = ranges[part]
        total = share(0, rows) + tok[0, rows].astype(jnp.float32)
        pl.when(inner)(direct(part, third, third, ahead(third)).wait_recv)
        for step in (crossing, 2):
            direct(part, step, step, ahead(step)).wait_recv()
        for step in range(1, n_col):
            total = total + incoming[step, rows].astype(jnp.float32)
        at = lax.broadcasted_iota(jnp.int32, (tall, 1), 0) + part * tall
        hidden[0, rows] = jnp.where(at < new_len[0], total, 0.0).astype(jnp.bfloat16)
    for step in range(1, n_col):
        pl.when(sends_own[step])(token_copies[step].wait_send)
    pl.when(inner)(forward.wait_send)
    for copy in key_copies[1:] + value_copies[1:] + page_copies + [direct(part, step, step, ahead(step)) for part in range(parts) for step in range(1, n_col)]:
        copy.wait_send()


def fused(
    tokens,
    w_query,
    w_key,
    w_value,
    w_out,
    diff_lambda,
    prefix_keys,
    prefix_values,
    new_len,
    prefix_len,
    holder,
    page_table,
):
    n_col, n_row, groups = lax.axis_size("col"), lax.axis_size("row"), lax.axis_size("grp")
    slots, cols = tokens.shape[1:]
    depth, wide = w_query.shape
    block = prefix_keys.shape[2]
    page = slots // groups
    maps = wide // DK
    scalars = pl.BlockSpec(memory_space=pltpu.SMEM)
    remains = pl.BlockSpec(memory_space=pltpu.HBM)
    whole = pl.BlockSpec(memory_space=pltpu.VMEM)
    half, full = jnp.bfloat16, jnp.float32
    return pl.pallas_call(
        functools.partial(kernel, n_col, n_row),
        out_shape=(
            jax.ShapeDtypeStruct((1, slots, cols), half),
            jax.ShapeDtypeStruct((1, 1, groups, page, wide), half),
            jax.ShapeDtypeStruct((1, 1, groups, page, wide), half),
        ),
        in_specs=[scalars] * 5 + [remains] * 7,
        out_specs=(whole, whole, whole),
        scratch_shapes=[
            pltpu.VMEM((n_col, slots, cols), half),
            pltpu.VMEM((3, depth, wide), half),
            pltpu.VMEM(w_out.shape, half),
            pltpu.VMEM((groups + 1, block, wide), half),
            pltpu.VMEM((groups + 1, block, wide), half),
            pltpu.VMEM((3, slots, wide), full),
            pltpu.VMEM((slots, wide), half),
            pltpu.VMEM((maps, slots, DV), full),
            pltpu.VMEM((maps, slots, 1), full),
            pltpu.VMEM((maps, slots, 1), full),
            pltpu.VMEM((slots, wide), half),
            pltpu.VMEM((n_col, slots, cols), half),
            pltpu.VMEM((n_col, slots, cols), half),
            pltpu.VMEM((2, slots, wide), half),
            pltpu.VMEM((2, groups, page, wide), half),
            pltpu.SemaphoreType.DMA((7,)),
            pltpu.SemaphoreType.DMA((n_col,)),
            pltpu.SemaphoreType.DMA((n_col,)),
            pltpu.SemaphoreType.DMA((2, groups)),
            pltpu.SemaphoreType.DMA((2, groups)),
            pltpu.SemaphoreType.DMA((2, groups)),
            pltpu.SemaphoreType.DMA((2, groups)),
            pltpu.SemaphoreType.DMA((n_col, 2)),
            pltpu.SemaphoreType.DMA((n_col, 2)),
        ],
        compiler_params=pltpu.CompilerParams(
            collective_id=0, has_side_effects=True, vmem_limit_bytes=56 << 20
        ),
    )(
        new_len,
        prefix_len,
        holder,
        page_table.T,
        diff_lambda,
        tokens,
        w_query,
        w_key,
        w_value,
        w_out,
        prefix_keys,
        prefix_values,
    )


def local(
    tokens,
    w_query,
    w_key,
    w_value,
    w_out,
    diff_lambda,
    prefix_keys,
    prefix_values,
    new_len,
    prefix_len,
    holder,
    page_table,
):
    if fits_kernel(w_query, prefix_keys):
        return fused(
            tokens,
            w_query,
            w_key,
            w_value,
            w_out,
            diff_lambda,
            prefix_keys,
            prefix_values,
            new_len,
            prefix_len,
            holder,
            page_table,
        )
    groups = lax.axis_size("grp")
    row_count = lax.axis_size("row")
    grp_index = lax.axis_index("grp")
    row_index = lax.axis_index("row")
    col_index = lax.axis_index("col")
    local_tokens = tokens[0]
    slot_count = local_tokens.shape[0]
    query_cols = w_query.shape[1]
    value_cols = w_value.shape[1]
    group_ids = jnp.arange(groups, dtype=jnp.int32)
    got_keys, got_values = (
        lax.all_to_all(prefix_keys[0], "grp", split_axis=0, concat_axis=0, tiled=True),
        lax.all_to_all(prefix_values[0], "grp", split_axis=0, concat_axis=0, tiled=True),
    )
    shard_piece = lax.all_gather(local_tokens, "col", axis=1, tiled=True)

    def partial_product(weight):
        return jnp.dot(shard_piece, weight, preferred_element_type=jnp.float32)

    as_float = shard_piece.astype(jnp.float32)
    query_sum = partial_product(w_query)
    key_sum = partial_product(w_key)
    value_sum = partial_product(w_value)
    square_sum = jnp.sum(as_float * as_float, axis=1)
    inv_rms = lax.rsqrt(square_sum / D + EPS_INPUT)[:, None]
    queries = (query_sum * inv_rms).astype(jnp.bfloat16)
    new_keys = (key_sum * inv_rms).astype(jnp.bfloat16)
    new_values = (value_sum * inv_rms).astype(jnp.bfloat16)
    is_live = jnp.arange(slot_count) < new_len[0]
    zero_entry = jnp.zeros((), jnp.bfloat16)
    page_size = slot_count // groups
    send_keys = jnp.where(is_live[:, None], new_keys, zero_entry).reshape(
        groups, page_size, query_cols
    )
    send_values = jnp.where(is_live[:, None], new_values, zero_entry).reshape(
        groups, page_size, value_cols
    )
    recv_keys, recv_values = (
        lax.all_to_all(send_keys, "grp", split_axis=0, concat_axis=0, tiled=True),
        lax.all_to_all(send_values, "grp", split_axis=0, concat_axis=0, tiled=True),
    )
    pick_block = (holder[0][:, None] == group_ids[None, :]).astype(jnp.bfloat16)
    fetched_keys = (
        jnp.einsum("bh,hpc->bpc", pick_block, got_keys, preferred_element_type=jnp.float32)
        .astype(jnp.bfloat16)
        .reshape(-1, query_cols)
    )
    fetched_values = (
        jnp.einsum("bh,hpc->bpc", pick_block, got_values, preferred_element_type=jnp.float32)
        .astype(jnp.bfloat16)
        .reshape(-1, value_cols)
    )
    prefix_span = fetched_keys.shape[0]
    position = jnp.arange(prefix_span + slot_count)
    within = jnp.arange(slot_count)
    allowed = jnp.where(
        position[None, :] < prefix_span,
        position[None, :] < prefix_len[0],
        position[None, :] - prefix_span <= within[:, None],
    )
    key_own = jnp.concatenate([fetched_keys, new_keys], axis=0)
    value_own = jnp.concatenate([fetched_values, new_values], axis=0)
    if query_cols == DK:
        is_first = col_index % 2 == 0
        head_lam = diff_lambda[col_index // 2]
        half_width = DV // 2
        partner_query, partner_key, partner_value, partner_pkey, partner_pvalue = swapped(
            (queries, new_keys, new_values, fetched_keys, fetched_values), "col", 0
        )
        query_zero, query_one = arrange(is_first, queries, partner_query)
        key_zero, key_one = arrange(
            is_first, key_own, jnp.concatenate([partner_pkey, partner_key], axis=0)
        )
        value_low, value_high = arrange(
            is_first, value_own, jnp.concatenate([partner_pvalue, partner_value], axis=0)
        )
        value_full = jnp.concatenate([value_low, value_high], axis=1)[:, None, :]
        map_zero = head_attend(query_zero[:, None, :], key_zero[:, None, :], value_full, allowed)
        map_one = head_attend(query_one[:, None, :], key_one[:, None, :], value_full, allowed)
        normed = head_norm(map_zero - head_lam * map_one)
        attended = lax.dynamic_slice_in_dim(
            normed[:, 0, :], col_index % 2 * half_width, half_width, 1
        ).astype(jnp.bfloat16)
    else:
        local_heads = query_cols // (2 * DK)
        query_four = queries.reshape(slot_count, local_heads, 2, DK)
        key_four = key_own.reshape(-1, local_heads, 2, DK)
        value_three = value_own.reshape(-1, local_heads, DV)
        map_zero = head_attend(query_four[:, :, 0], key_four[:, :, 0], value_three, allowed)
        map_one = head_attend(query_four[:, :, 1], key_four[:, :, 1], value_three, allowed)
        head_lam = lax.dynamic_slice_in_dim(diff_lambda, col_index * local_heads, local_heads, 0)
        normed = head_norm(map_zero - head_lam[None, :, None] * map_one)
        attended = normed.reshape(slot_count, local_heads * DV).astype(jnp.bfloat16)
    mixed = lax.psum_scatter(
        lax.dot_general(
            w_out, attended, (((0,), (1,)), ((), ())), preferred_element_type=jnp.float32
        ),
        "col",
        scatter_dimension=0,
        tiled=True,
    ).T
    combined = local_tokens.astype(jnp.float32) + mixed
    hidden = jnp.where(is_live[:, None], combined, 0.0).astype(jnp.bfloat16)[None]
    sources = group_ids * row_count + row_index
    slot_of = page_table[sources, grp_index]
    placement_map = (slot_of[None, :] == group_ids[:, None]).astype(jnp.bfloat16)
    page_keys = jnp.einsum(
        "sg,gpc->spc", placement_map, recv_keys, preferred_element_type=jnp.float32
    ).astype(jnp.bfloat16)[None, None]
    page_values = jnp.einsum(
        "sg,gpc->spc", placement_map, recv_values, preferred_element_type=jnp.float32
    ).astype(jnp.bfloat16)[None, None]
    return (hidden, page_keys, page_values)


def solution(mesh):
    placed = (
        P(("grp", "row"), None, "col"),
        P(None, "col"),
        P(None, "col"),
        P(None, "col"),
        P("col", None),
        P(),
        P(("grp", "row"), None, None, "col"),
        P(("grp", "row"), None, None, "col"),
        P(("grp", "row")),
        P(("grp", "row")),
        P(("grp", "row"), None),
        P(),
    )
    return jax.shard_map(
        local,
        mesh=mesh,
        in_specs=placed,
        out_specs=(
            P(("grp", "row"), None, "col"),
            P("grp", "row", None, None, "col"),
            P("grp", "row", None, None, "col"),
        ),
        check_vma=False,
    )
```
